256 devices in a mesh: ball: 16 (over y, x), region: 16 (over z, core).
Axes of the slice: x: 4, y: 4, z: 8, core: 2. Of those that a mesh axis runs over, the one named last changes fastest.
Arguments:
- points: bfloat16 [16, 16, 1024, 256], P('ball', 'region'), may hold values from -6 to 6
- gain_attn: float32 [256], replicated, may hold values from 0.1 to 1.9
- w_query_key: bfloat16 [256, 512], replicated, may hold values from -7 to 7
- w_value: bfloat16 [256, 256], replicated, may hold values from -0.375 to 0.375
- w_out: bfloat16 [256, 256], replicated, may hold values from -0.375 to 0.375
- gain_mlp: float32 [256], replicated, may hold values from 0.1 to 1.9
- w_up: bfloat16 [256, 1024], replicated, may hold values from -0.375 to 0.375
- w_down: bfloat16 [1024, 256], replicated, may hold values from -0.1875 to 0.1875
- cluster_dest: int32 [16, 16, 16], P('ball', 'region'), may hold values from 0 to 255, as said below
Outputs:
- block_out: bfloat16 [16, 16, 1024, 256], P('ball', 'region')
The draws below stay inside these ranges and needn't reach their ends.
Inputs may be any that keep to these rules, and one draw needn't show every extreme that they name: cluster_dest[l, r, c] = o * 16 + s sends cluster c of lane l, region r to slot s of lane o, region r. Within one region all values are distinct. Each lane sends exactly 2 clusters to each of 8 owner lanes and none to the others, and the offsets (o - l) mod 16 of those owners are the same set for every lane of one region.
All inputs are finite; a program needn't handle non-finite values.
Results may differ from the reference program's by a relative error of at most 0.012.
The reference program's roundings to bfloat16 on the way count: a program that leaves them out, or rounds other values in their place, can miss the bound.
Values may be sent and summed in bfloat16 or wider, within the bound.
A program may use at most 64 MiB of HBM per device.

```python
import math
import jax
import jax.numpy as jnp
from jax import lax

C = 256
HEADS = 8
MLP_HID = 1024
BALL = 1024
CLUSTER = 64
POOL = 16
PTS_DEV = 1024
CLUS_DEV = 16
LANES = 16
REGIONS = 16
CAP = 2


def draw_points(key, part):
    shape = (LANES, REGIONS, PTS_DEV, C)
    key_base = jax.random.fold_in(key, 0)
    base = jax.random.normal(key_base, shape, jnp.float32)
    return jnp.clip(base, -6.0, 6.0).astype(jnp.bfloat16)


def draw_w_query_key(key, part):
    key_query, key_keys = jax.random.split(key, 2)
    factor = 2.0 / math.sqrt(C)
    query_part = jnp.clip(jax.random.normal(key_query, (C, C), jnp.float32), -4.0, 4.0) * factor
    key_part = jnp.clip(jax.random.normal(key_keys, (C, C), jnp.float32), -4.0, 4.0) * factor
    return jnp.clip(jnp.concatenate([query_part, key_part], axis=1), -7.0, 7.0).astype(jnp.bfloat16)


def draw_cluster_dest(key, part):
    half = LANES // 2
    key_offsets, key_order, key_slots = jax.random.split(key, 3)
    offset_scores = jax.random.randint(key_offsets, (REGIONS, LANES), 0, 1 << 20) * LANES + jnp.arange(LANES, dtype=jnp.int32)[None, :]
    chosen = jnp.sort(jnp.argsort(offset_scores, axis=1)[:, :half], axis=1).astype(jnp.int32)
    region_ids = jnp.arange(REGIONS, dtype=jnp.int32)[:, None]
    member = jnp.zeros((REGIONS, LANES), jnp.int32).at[region_ids, chosen].set(1)
    sources = jnp.arange(LANES, dtype=jnp.int32)
    offsets_table = (sources[None, :] - sources[:, None]) % LANES
    sends = member[:, offsets_table]
    source_rank = jnp.cumsum(sends, axis=1) - sends
    order_scores = jax.random.randint(key_order, (REGIONS, LANES, CLUS_DEV), 0, 1 << 20) * CLUS_DEV + jnp.arange(CLUS_DEV, dtype=jnp.int32)
    position = jnp.argsort(jnp.argsort(order_scores, axis=2), axis=2).astype(jnp.int32)
    chosen_wide = jnp.broadcast_to(chosen[:, None, :], (REGIONS, LANES, half))
    offset = jnp.take_along_axis(chosen_wide, position // CAP, axis=2)
    owner = (sources[None, :, None] + offset) % LANES
    within = position % CAP
    arrival = jnp.take_along_axis(source_rank, owner, axis=2) * CAP + within
    slot_scores = jax.random.randint(key_slots, (REGIONS, LANES, CLUS_DEV), 0, 1 << 20) * CLUS_DEV + jnp.arange(CLUS_DEV, dtype=jnp.int32)
    slot_perm = jnp.argsort(slot_scores, axis=2).astype(jnp.int32).reshape(REGIONS, LANES * CLUS_DEV)
    slot_index = (owner * CLUS_DEV + arrival).reshape(REGIONS, LANES * CLUS_DEV)
    slots = jnp.take_along_axis(slot_perm, slot_index, axis=1).reshape(REGIONS, LANES, CLUS_DEV)
    destination = owner * CLUS_DEV + slots
    return destination.transpose(1, 0, 2).astype(jnp.int32)


def gaussian(key, dims, spread, limit, held_as=jnp.bfloat16):
    entries = jax.random.normal(key, dims, jnp.float32) * spread
    return jnp.minimum(jnp.maximum(entries, -limit), limit).astype(held_as)


def setup_inputs(seed: int = 0) -> dict:
    key_list = jax.random.split(jax.random.key(seed), 10)
    return {
        "points": draw_points(jax.random.fold_in(key_list[9], 71), 0),
        "gain_attn": jnp.clip(1.0 + 0.18 * jax.random.normal(key_list[1], (C,), jnp.float32), 0.1, 1.9),
        "w_query_key": draw_w_query_key(jax.random.fold_in(key_list[9], 71), 0),
        "w_value": gaussian(key_list[3], (C, C), C ** -0.5, 0.375),
        "w_out": gaussian(key_list[4], (C, C), C ** -0.5, 0.375),
        "gain_mlp": jnp.clip(1.0 + 0.18 * jax.random.normal(key_list[5], (C,), jnp.float32), 0.1, 1.9),
        "w_up": gaussian(key_list[6], (C, MLP_HID), C ** -0.5, 0.375),
        "w_down": gaussian(key_list[7], (MLP_HID, C), MLP_HID ** -0.5, 0.1875),
        "cluster_dest": draw_cluster_dest(jax.random.fold_in(key_list[9], 71), 0),
    }


def rms_norm(row_data, gain_vector):
    widened = row_data.astype(jnp.float32)
    scaling = lax.rsqrt(lax.optimization_barrier(jnp.mean(widened * widened, axis=1, keepdims=True)) + 1e-06)
    return (widened * scaling * gain_vector.astype(jnp.float32)).astype(jnp.bfloat16)

def attend(query, keys, values):
    row_count, columns = query.shape
    head_size = columns // HEADS
    row_block = min(512, row_count)
    query_heads = query.reshape(row_count // row_block, row_block, HEADS, head_size).transpose(2, 0, 1, 3)
    key_heads = keys.reshape(-1, HEADS, head_size).transpose(1, 0, 2)
    value_heads = values.reshape(-1, HEADS, head_size).transpose(1, 0, 2)

    def one_head(operands):
        query_blocks, key_head, value_head = operands

        def one_block(query_block):
            scores = jnp.einsum('nd,md->nm', query_block.astype(jnp.float32), key_head.astype(jnp.float32)) / math.sqrt(head_size)
            row_max = lax.optimization_barrier(jnp.max(scores, axis=1, keepdims=True))
            exponent = jnp.exp(scores - row_max)
            weights = (exponent / lax.optimization_barrier(jnp.sum(exponent, axis=1, keepdims=True))).astype(jnp.bfloat16)
            mixed = jnp.einsum('nm,md->nd', weights.astype(jnp.float32), value_head.astype(jnp.float32))
            return mixed.astype(jnp.bfloat16)
        return lax.map(one_block, query_blocks)
    result = lax.map(one_head, (query_heads, key_heads, value_heads))
    return result.transpose(1, 2, 0, 3).reshape(row_count, columns)

def reference(points, gain_attn, w_query_key, w_value, w_out, gain_mlp, w_up, w_down, cluster_dest):
    lanes, regions, per_device, columns = points.shape
    clusters = per_device // CLUSTER
    flat = points.reshape(-1, columns)
    normed = rms_norm(flat, gain_attn)
    paired = jnp.dot(normed, w_query_key, preferred_element_type=jnp.float32).astype(jnp.bfloat16)
    query = paired[:, :columns]
    keys = paired[:, columns:]
    values = jnp.dot(normed, w_value, preferred_element_type=jnp.float32).astype(jnp.bfloat16)

    def pooled(source):
        summed = lax.optimization_barrier(jnp.sum(source.reshape(-1, POOL, columns).astype(jnp.float32), axis=1))
        return (summed / math.sqrt(POOL)).astype(jnp.bfloat16).reshape(lanes, -1, columns)
    pooled_keys = pooled(keys)
    pooled_values = pooled(values)
    ball_count = flat.shape[0] // BALL
    per_lane = ball_count // lanes
    ball_indices = jnp.arange(ball_count, dtype=jnp.int32)

    def near_ball(index):
        start = index * BALL
        lane = index // per_lane
        ball_query = lax.dynamic_slice_in_dim(query, start, BALL, 0)
        ball_keys = lax.dynamic_slice_in_dim(keys, start, BALL, 0)
        ball_values = lax.dynamic_slice_in_dim(values, start, BALL, 0)
        lane_keys = lax.dynamic_index_in_dim(pooled_keys, lane, 0, keepdims=False)
        lane_values = lax.dynamic_index_in_dim(pooled_values, lane, 0, keepdims=False)
        return attend(ball_query, jnp.concatenate([ball_keys, lane_keys], axis=0), jnp.concatenate([ball_values, lane_values], axis=0))
    near = lax.map(near_ball, ball_indices).reshape(-1, columns)

    def by_region(source):
        inner = source.shape[1]
        return source.reshape(lanes, regions, clusters, CLUSTER * inner).transpose(1, 0, 2, 3).reshape(regions, lanes * clusters, CLUSTER * inner)

    def from_region(source, inner):
        return source.reshape(regions, lanes, clusters, CLUSTER * inner).transpose(1, 0, 2, 3).reshape(-1, inner)
    target = cluster_dest.transpose(1, 0, 2).reshape(regions, lanes * clusters).astype(jnp.int32)
    stacked = by_region(jnp.concatenate([query, keys, values], axis=1))
    placed = jax.vmap(lambda where_to, source: jnp.zeros_like(source).at[where_to].set(source))(target, stacked)
    rotated = from_region(placed, 3 * columns)

    def far_ball(index):
        ball_rows = lax.dynamic_slice_in_dim(rotated, index * BALL, BALL, 0)
        return attend(ball_rows[:, :columns], ball_rows[:, columns:2 * columns], ball_rows[:, 2 * columns:])
    far_rotated = lax.map(far_ball, ball_indices).reshape(-1, columns)
    far = from_region(jax.vmap(lambda where_to, source: source[where_to])(target, by_region(far_rotated)), columns)
    after = (flat.astype(jnp.float32) + jnp.dot(near, w_out, preferred_element_type=jnp.float32) + jnp.dot(far, w_out, preferred_element_type=jnp.float32)).astype(jnp.bfloat16)
    normed_mlp = rms_norm(after, gain_mlp)
    hidden = jax.nn.gelu(jnp.dot(normed_mlp, w_up, preferred_element_type=jnp.float32), approximate=True).astype(jnp.bfloat16)
    block_out = (after.astype(jnp.float32) + jnp.dot(hidden, w_down, preferred_element_type=jnp.float32)).astype(jnp.bfloat16)
    return block_out.reshape(points.shape)
```

```python
import functools
import math

import jax
import jax.numpy as jnp
from jax import lax
from jax.experimental import pallas as pl
from jax.experimental.pallas import tpu as pltpu
from jax.sharding import PartitionSpec as P

MESH = pl.DeviceIdType.MESH
BF = jnp.bfloat16
F32 = jnp.float32
HEADS = 8
HEAD = 32
C = 256
ROWS = 1024
CLUSTER = 64
CLUSTERS = 16
LANES = 16
POOL = 16
POOLED = ROWS // POOL
CHIPS = 8
QB = 512
QBLOCKS = ROWS // QB
ROW_CHUNK = 256
SCALE = math.log2(math.e) / math.sqrt(HEAD)


def norm_rows(x, gain):
    x = x.astype(F32)
    scale = lax.rsqrt(jnp.mean(x * x, axis=1, keepdims=True) + 1e-6)
    return (x * scale * gain).astype(BF)


def kernel(
    dest, x_ref, gain_a, wqk, wv, wout, gain_m, wup, wdown, out,
    normed, settled, qz, far_qz, keys, vals, pool, pvals, score, near_sum, near_max, near_t, far_t,
    send, recv, back_send, back_recv,
    out_sems, in_sems, bout_sems, bin_sems, pout_sems, pin_sems,
):
    me = lax.axis_index("ball")
    spot = lax.axis_index("region")
    chip, core = spot // 2, spot % 2

    def lane(offset):
        return {"ball": lax.rem(me + offset + LANES, LANES)}

    def chip_at(offset):
        return {"region": lax.rem(chip + offset + CHIPS, CHIPS) * 2 + core}

    partner = {"region": chip * 2 + 1 - core}

    barrier = pltpu.get_barrier_semaphore()
    for d in range(1, LANES):
        pl.semaphore_signal(barrier, inc=1, device_id=lane(d), device_id_type=MESH)
    for d in range(1, CHIPS):
        pl.semaphore_signal(barrier, inc=1, device_id=chip_at(d), device_id_type=MESH)
    pl.semaphore_signal(barrier, inc=1, device_id=partner, device_id_type=MESH)

    offsets = [lax.bitwise_and((dest[c] // CLUSTERS) - me + LANES, LANES - 1) for c in range(CLUSTERS)]
    first, second, active, upto = [], [], [], []
    count = jnp.int32(0)
    for d in range(LANES):
        lo, hi, hit = jnp.int32(CLUSTERS - 1), jnp.int32(0), jnp.int32(0)
        for c in range(CLUSTERS):
            same = offsets[c] == d
            lo = jnp.minimum(lo, jnp.where(same, c, CLUSTERS - 1))
            hi = jnp.maximum(hi, jnp.where(same, c, 0))
            hit = jnp.maximum(hit, jnp.where(same, 1, 0))
        count = count + hit
        first.append(lo)
        second.append(hi)
        active.append(hit)
        upto.append(count)

    def norm_chunk(i, _):
        n = norm_rows(x_ref[pl.ds(pl.multiple_of(i * ROW_CHUNK, ROW_CHUNK), ROW_CHUNK), :], gain_a[...])
        normed[pl.ds(i * (ROW_CHUNK // CLUSTER), ROW_CHUNK // CLUSTER)] = n.reshape(
            ROW_CHUNK // CLUSTER, CLUSTER, C
        )
        return 0

    lax.fori_loop(0, ROWS // ROW_CHUNK, norm_chunk, 0)
    for d in range(LANES):
        held = recv if d == 0 else send
        held[2 * d] = normed[first[d]]
        held[2 * d + 1] = normed[second[d]]

    pl.semaphore_wait(barrier, LANES - 1 + CHIPS - 1 + 1)
    sends = []
    for d in range(1, LANES):
        copy = pltpu.make_async_remote_copy(
            src_ref=send.at[pl.ds(2 * d, 2)], dst_ref=recv.at[pl.ds(2 * d, 2)],
            send_sem=out_sems.at[d], recv_sem=in_sems.at[d], device_id=lane(d), device_id_type=MESH,
        )
        copy.start()
        sends.append(copy)

    def project(source, qz):
        states = source[...].reshape(ROWS, C)
        turned = states.T
        query_t = jnp.dot(wqk[:, :C].T, turned, preferred_element_type=F32).astype(BF)
        for h in range(HEADS):
            at = h % 4 * HEAD
            qz[h, at:at + HEAD, :] = query_t[h * HEAD:(h + 1) * HEAD, :]
        keys[...] = jnp.dot(states, wqk[:, C:], preferred_element_type=F32).astype(BF)
        value_t = jnp.dot(wv[...].T, turned, preferred_element_type=F32).astype(BF)
        for h in range(HEADS):
            vals[h, :HEAD, :] = value_t[h * HEAD:(h + 1) * HEAD, :]

    qz[...] = jnp.zeros_like(qz)
    far_qz[...] = jnp.zeros_like(far_qz)
    for h in range(HEADS):
        vals[h, HEAD:, :] = jnp.ones((16, ROWS), BF)
        pvals[h, HEAD:, :] = jnp.ones((16, ROWS), BF)
    project(normed, qz)

    row = lax.broadcasted_iota(jnp.int32, (POOLED, ROWS), 0)
    col = lax.broadcasted_iota(jnp.int32, (POOLED, ROWS), 1)
    pooling = jnp.where(col // POOL == row, 1.0 / math.sqrt(POOL), 0.0).astype(BF)
    pool[:POOLED, :C] = jnp.dot(pooling, keys[...], preferred_element_type=F32).astype(BF)
    value_rows = jnp.dot(normed[...].reshape(ROWS, C), wv[...], preferred_element_type=F32).astype(BF)
    pool[:POOLED, C:] = jnp.dot(pooling, value_rows, preferred_element_type=F32).astype(BF)
    pooled_sends = []
    for d in range(1, CHIPS):
        copy = pltpu.make_async_remote_copy(
            src_ref=pool.at[pl.ds(0, POOLED)], dst_ref=pool.at[pl.ds(d * POOLED, POOLED)],
            send_sem=pout_sems.at[d], recv_sem=pin_sems.at[d], device_id=chip_at(d), device_id_type=MESH,
        )
        copy.start()
        pooled_sends.append(copy)

    def attend(qz, key_ref, value_ref, finish):
        def block(i, _):
            h, b = i // QBLOCKS, i % QBLOCKS
            cols = pl.ds(pl.multiple_of(b * QB, QB), QB)
            top = jnp.full((8, QB), -jnp.inf, F32)
            for c in range(ROWS // ROW_CHUNK):
                rows = pl.ds(c * ROW_CHUNK, ROW_CHUNK)
                k = key_ref[rows, pl.ds(pl.multiple_of(h // 4 * 128, 128), 128)]
                s = jnp.dot(k, qz[h, :, cols], preferred_element_type=F32)
                score[rows, :] = s
                for j in range(ROW_CHUNK // 8):
                    top = jnp.maximum(top, s[j * 8:(j + 1) * 8])
            top = jnp.max(top, axis=0, keepdims=True)
            total = jnp.zeros((48, QB), F32)
            for c in range(ROWS // ROW_CHUNK):
                rows = pl.ds(c * ROW_CHUNK, ROW_CHUNK)
                p = jnp.exp2((score[rows, :] - top) * SCALE).astype(BF)
                total = total + jnp.dot(value_ref[h, :, rows], p, preferred_element_type=F32)
            finish(h, cols, top, total)
            return 0

        lax.fori_loop(0, HEADS * QBLOCKS, block, 0)

    def keep(h, cols, top, total):
        near_sum[h, :, cols] = total
        near_max[h, :, cols] = jnp.broadcast_to(top, (8, QB))

    def head_rows(h):
        return pl.ds(pl.multiple_of(h * HEAD, HEAD), HEAD)

    def close(total):
        return (total[:HEAD] / total[HEAD:HEAD + 1]).astype(BF)

    def merge(h, cols, top, total):
        before = near_max[h, :1, cols]
        both = jnp.maximum(before, top)
        whole = near_sum[h, :, cols] * jnp.exp2((before - both) * SCALE) + total * jnp.exp2((top - both) * SCALE)
        near_t[head_rows(h), cols] = close(whole)

    def far_done(h, cols, top, total):
        far_t[head_rows(h), cols] = close(total)

    attend(qz, keys, vals, keep)

    for copy in pooled_sends:
        copy.wait()
    across = pltpu.make_async_remote_copy(
        src_ref=pool.at[pl.ds(0, ROWS // 2)], dst_ref=pool.at[pl.ds(ROWS // 2, ROWS // 2)],
        send_sem=pout_sems.at[0], recv_sem=pin_sems.at[0], device_id=partner, device_id_type=MESH,
    )
    across.start()

    for copy in sends:
        copy.wait()
    for j in range(LANES // 2):
        d = jnp.int32(0)
        for k in range(LANES):
            d = d + jnp.where(upto[k] <= j, 1, 0)
        d = jnp.minimum(d, LANES - 1)
        settled[2 * j] = recv[2 * d]
        settled[2 * j + 1] = recv[2 * d + 1]
    project(settled, far_qz)
    attend(far_qz, keys, vals, far_done)
    settled[...] = far_t[...].T.reshape(CLUSTERS, CLUSTER, C)
    for d in range(LANES):
        held = back_recv if d == 0 else back_send
        j = jnp.minimum(upto[d] - active[d], LANES // 2 - 1)
        held[2 * d] = settled[2 * j]
        held[2 * d + 1] = settled[2 * j + 1]
    backs = []
    for d in range(1, LANES):
        copy = pltpu.make_async_remote_copy(
            src_ref=back_send.at[pl.ds(2 * d, 2)], dst_ref=back_recv.at[pl.ds(2 * d, 2)],
            send_sem=bout_sems.at[d], recv_sem=bin_sems.at[d], device_id=lane(-d), device_id_type=MESH,
        )
        copy.start()
        backs.append(copy)

    across.wait()
    turned = pool[:, C:].T
    for h in range(HEADS):
        pvals[h, :HEAD, :] = turned[h * HEAD:(h + 1) * HEAD, :]
    attend(qz, pool, pvals, merge)

    for copy in backs:
        copy.wait()
    for c in range(CLUSTERS):
        rank = jnp.int32(0)
        for e in range(c):
            rank = rank + jnp.where(offsets[e] == offsets[c], 1, 0)
        settled[c] = back_recv[2 * offsets[c] + jnp.minimum(rank, 1)]

    def tail(i, _):
        rows = pl.ds(pl.multiple_of(i * ROW_CHUNK, ROW_CHUNK), ROW_CHUNK)
        near = near_t[:, rows].T
        far = settled[pl.ds(i * (ROW_CHUNK // CLUSTER), ROW_CHUNK // CLUSTER)].reshape(ROW_CHUNK, C)
        after = (
            x_ref[rows, :].astype(F32)
            + jnp.dot(near, wout[...], preferred_element_type=F32)
            + jnp.dot(far, wout[...], preferred_element_type=F32)
        ).astype(BF)
        mlp_in = norm_rows(after, gain_m[...])
        hidden = jax.nn.gelu(jnp.dot(mlp_in, wup[...], preferred_element_type=F32), approximate=True).astype(BF)
        out[rows, :] = (
            after.astype(F32) + jnp.dot(hidden, wdown[...], preferred_element_type=F32)
        ).astype(BF)
        return 0

    lax.fori_loop(0, ROWS // ROW_CHUNK, tail, 0)


def per_device(points, gain_attn, w_query_key, w_value, w_out, gain_mlp, w_up, w_down, cluster_dest):
    vmem = pl.BlockSpec(memory_space=pltpu.VMEM)
    clusters = pltpu.VMEM((CLUSTERS, CLUSTER, C), BF)
    slots = pltpu.VMEM((2 * LANES, CLUSTER, C), BF)
    values = pltpu.VMEM((HEADS, 48, ROWS), BF)
    turned = pltpu.VMEM((C, ROWS), BF)
    result = pl.pallas_call(
        kernel,
        out_shape=jax.ShapeDtypeStruct((ROWS, C), BF),
        in_specs=[pl.BlockSpec(memory_space=pltpu.SMEM)] + [vmem] * 8,
        out_specs=vmem,
        scratch_shapes=[
            clusters, clusters,
            pltpu.VMEM((HEADS, 128, ROWS), BF),
            pltpu.VMEM((HEADS, 128, ROWS), BF),
            pltpu.VMEM((ROWS, C), BF),
            values,
            pltpu.VMEM((ROWS, 2 * C), BF),
            values,
            pltpu.VMEM((ROWS, QB), F32),
            pltpu.VMEM((HEADS, 48, ROWS), F32),
            pltpu.VMEM((HEADS, 8, ROWS), F32),
            turned, turned,
            slots, slots, slots, slots,
        ]
        + [pltpu.SemaphoreType.DMA((LANES,))] * 4
        + [pltpu.SemaphoreType.DMA((CHIPS,))] * 2,
        compiler_params=pltpu.CompilerParams(
            collective_id=0, has_side_effects=True, vmem_limit_bytes=60 * 1024 * 1024
        ),
        name="block",
    )(
        cluster_dest.reshape(CLUSTERS), points.reshape(ROWS, C), gain_attn.reshape(1, C), w_query_key,
        w_value, w_out, gain_mlp.reshape(1, C), w_up, w_down,
    )
    return result.reshape(points.shape)


def solution(mesh):
    placed = (P("ball", "region", None, None),) + (P(),) * 7 + (P("ball", "region", None),)
    return jax.shard_map(
        per_device, mesh=mesh, in_specs=placed, out_specs=P("ball", "region", None, None), check_vma=False
    )
```

```python
import functools
import math

import jax
import jax.numpy as jnp
from jax import lax
from jax.experimental import pallas as pl
from jax.experimental.pallas import tpu as pltpu
from jax.sharding import PartitionSpec as P

MESH = pl.DeviceIdType.MESH
BF = jnp.bfloat16
F32 = jnp.float32
HEADS = 8
HEAD = 32
C = 256
ROWS = 1024
CLUSTER = 64
CLUSTERS = 16
LANES = 16
POOL = 16
POOLED = ROWS // POOL
CHIPS = 8
QB = 512
QBLOCKS = ROWS // QB
BLOCKS = HEADS * QBLOCKS
GROUP = 2
PIECE = 128
DEPTH = 256
ROW_CHUNK = 256
SCALE = math.log2(math.e) / math.sqrt(HEAD)


def norm_rows(x, gain):
    x = x.astype(F32)
    scale = lax.rsqrt(jnp.mean(x * x, axis=1, keepdims=True) + 1e-6)
    return (x * scale * gain).astype(BF)


def kernel(
    dest, x_ref, gain_a, wqk, wv, wout, gain_m, wup, wdown, out,
    normed, settled, near_q, far_q, keys, vals, pool, score, weight, tops, near_sum, near_max, near_t, far_t,
    send, recv, back_send, back_recv,
    out_sems, in_sems, bout_sems, bin_sems, pout_sems, pin_sems,
):
    me = lax.axis_index("ball")
    spot = lax.axis_index("region")
    chip, core = spot // 2, spot % 2

    def lane(offset):
        return {"ball": lax.rem(me + offset + LANES, LANES)}

    def chip_at(offset):
        return {"region": lax.rem(chip + offset + CHIPS, CHIPS) * 2 + core}

    partner = {"region": chip * 2 + 1 - core}

    barrier = pltpu.get_barrier_semaphore()
    for d in range(1, LANES):
        pl.semaphore_signal(barrier, inc=1, device_id=lane(d), device_id_type=MESH)
    for d in range(1, CHIPS):
        pl.semaphore_signal(barrier, inc=1, device_id=chip_at(d), device_id_type=MESH)
    pl.semaphore_signal(barrier, inc=1, device_id=partner, device_id_type=MESH)

    offsets = [lax.bitwise_and(lax.shift_right_arithmetic(dest[c], 4) - me, LANES - 1) for c in range(CLUSTERS)]
    first, second, active, upto = [], [], [], []
    count = jnp.int32(0)
    for d in range(LANES):
        lo, hi = jnp.int32(CLUSTERS), jnp.int32(0)
        for c in range(CLUSTERS):
            hi = jnp.where(offsets[c] == d, c, hi)
            lo = jnp.where(offsets[CLUSTERS - 1 - c] == d, CLUSTERS - 1 - c, lo)
        hit = jnp.where(lo < CLUSTERS, 1, 0)
        count = count + hit
        first.append(jnp.minimum(lo, CLUSTERS - 1))
        second.append(hi)
        active.append(hit)
        upto.append(count)

    def norm_chunk(i, _):
        n = norm_rows(x_ref[pl.ds(pl.multiple_of(i * ROW_CHUNK, ROW_CHUNK), ROW_CHUNK), :], gain_a[...])
        normed[pl.ds(i * (ROW_CHUNK // CLUSTER), ROW_CHUNK // CLUSTER)] = n.reshape(
            ROW_CHUNK // CLUSTER, CLUSTER, C
        )
        return 0

    lax.fori_loop(0, ROWS // ROW_CHUNK, norm_chunk, 0)
    for d in range(LANES):
        held = recv if d == 0 else send
        held[2 * d] = normed[first[d]]
        held[2 * d + 1] = normed[second[d]]

    pl.semaphore_wait(barrier, LANES - 1 + CHIPS - 1 + 1)
    sends = []
    for d in range(1, LANES):
        copy = pltpu.make_async_remote_copy(
            src_ref=send.at[pl.ds(2 * d, 2)], dst_ref=recv.at[pl.ds(2 * d, 2)],
            send_sem=out_sems.at[d], recv_sem=in_sems.at[d], device_id=lane(d), device_id_type=MESH,
        )
        copy.start()
        sends.append(copy)

    def set_keys(rows):
        for h in range(HEADS):
            keys[h] = rows[:, h * HEAD:(h + 1) * HEAD]

    def set_values(value_t):
        for h in range(HEADS):
            vals[h, :HEAD, :] = value_t[h * HEAD:(h + 1) * HEAD, :]

    def project(source, query_t):
        states = source[...].reshape(ROWS, C)
        turned = states.T
        query_t[...] = jnp.dot(wqk[:, :C].T, turned, preferred_element_type=F32).astype(BF)
        key_rows = jnp.dot(states, wqk[:, C:], preferred_element_type=F32).astype(BF)
        set_keys(key_rows)
        set_values(jnp.dot(wv[...].T, turned, preferred_element_type=F32).astype(BF))
        return key_rows

    for h in range(HEADS):
        vals[h, HEAD:, :] = jnp.ones((16, ROWS), BF)
    key_rows = project(normed, near_q)

    row = lax.broadcasted_iota(jnp.int32, (POOLED, ROWS), 0)
    col = lax.broadcasted_iota(jnp.int32, (POOLED, ROWS), 1)
    pooling = jnp.where(col // POOL == row, 1.0 / math.sqrt(POOL), 0.0).astype(BF)
    pool[:POOLED, :C] = jnp.dot(pooling, key_rows, preferred_element_type=F32).astype(BF)
    value_rows = jnp.dot(normed[...].reshape(ROWS, C), wv[...], preferred_element_type=F32).astype(BF)
    pool[:POOLED, C:] = jnp.dot(pooling, value_rows, preferred_element_type=F32).astype(BF)
    pooled_sends = []
    for d in range(1, CHIPS):
        copy = pltpu.make_async_remote_copy(
            src_ref=pool.at[pl.ds(0, POOLED)], dst_ref=pool.at[pl.ds(d * POOLED, POOLED)],
            send_sem=pout_sems.at[d], recv_sem=pin_sems.at[d], device_id=chip_at(d), device_id_type=MESH,
        )
        copy.start()
        pooled_sends.append(copy)

    def attend(query_t, finish):
        def spot_of(i):
            return i // QBLOCKS, pl.ds(pl.multiple_of(i % QBLOCKS * QB, QB), QB)

        def head_rows(h):
            return pl.ds(pl.multiple_of(h * HEAD, HEAD), HEAD)

        def scores_of(i, slot, r, top):
            h, cols = spot_of(i)
            rows = pl.ds(r * PIECE, PIECE)
            s = jnp.dot(keys[h, rows, :], query_t[head_rows(h), cols], preferred_element_type=F32)
            score[slot, rows, :] = s
            for j in range(PIECE // 8):
                top = jnp.maximum(top, s[j * 8:(j + 1) * 8])
            return top

        def sum_of(h, slot, c, total):
            rows = pl.ds(c * DEPTH, DEPTH)
            return total + jnp.dot(vals[h, :, rows], weight[slot, rows, :], preferred_element_type=F32)

        def top_of(slot):
            return jnp.max(tops[slot], axis=0, keepdims=True)

        low = jnp.full((8, QB), -jnp.inf, F32)
        none = jnp.zeros((48, QB), F32)

        def step(g, even):
            for b in range(GROUP):
                i = g * GROUP + b
                now = b if even else GROUP + b
                other = GROUP + b if even else b
                old = jnp.maximum(i - GROUP, 0)
                new = jnp.minimum(i + GROUP, BLOCKS - 1)
                old_head, old_cols = spot_of(old)
                old_top = top_of(other)
                top = top_of(now)
                new_top, total = low, none
                for r in range(ROWS // PIECE):
                    rows = pl.ds(r * PIECE, PIECE)
                    new_top = scores_of(new, other, r, new_top)
                    weight[now, rows, :] = jnp.exp2((score[now, rows, :] - top) * SCALE).astype(BF)
                    if (r + 1) * PIECE % DEPTH == 0:
                        total = sum_of(old_head, other, (r + 1) * PIECE // DEPTH - 1, total)
                tops[other] = new_top
                finish(old_head, old_cols, old_top, total)

        for b in range(GROUP):
            top = low
            for r in range(ROWS // PIECE):
                top = scores_of(b, b, r, top)
            tops[b] = top

        def pair(t, _):
            @pl.when(2 * t < BLOCKS // GROUP)
            def _():
                step(2 * t, True)

            @pl.when(2 * t + 1 < BLOCKS // GROUP)
            def _():
                step(2 * t + 1, False)

            return 0

        lax.fori_loop(0, BLOCKS // GROUP // 2, pair, 0)
        for b in range(GROUP):
            h, cols = spot_of(BLOCKS - GROUP + b)
            total = none
            for c in range(ROWS // DEPTH):
                total = sum_of(h, GROUP + b, c, total)
            finish(h, cols, top_of(GROUP + b), total)

    def keep(h, cols, top, total):
        near_sum[h, :, cols] = total
        near_max[h, :, cols] = jnp.broadcast_to(top, (8, QB))

    def head_rows(h):
        return pl.ds(pl.multiple_of(h * HEAD, HEAD), HEAD)

    def close(total):
        return (total[:HEAD] / total[HEAD:HEAD + 1]).astype(BF)

    def merge(h, cols, top, total):
        before = near_max[h, :1, cols]
        both = jnp.maximum(before, top)
        whole = near_sum[h, :, cols] * jnp.exp2((before - both) * SCALE) + total * jnp.exp2((top - both) * SCALE)
        near_t[head_rows(h), cols] = close(whole)

    def far_done(h, cols, top, total):
        far_t[head_rows(h), cols] = close(total)

    attend(near_q, keep)

    for copy in pooled_sends:
        copy.wait()
    across = pltpu.make_async_remote_copy(
        src_ref=pool.at[pl.ds(0, ROWS // 2)], dst_ref=pool.at[pl.ds(ROWS // 2, ROWS // 2)],
        send_sem=pout_sems.at[0], recv_sem=pin_sems.at[0], device_id=partner, device_id_type=MESH,
    )
    across.start()

    for copy in sends:
        copy.wait()
    for j in range(LANES // 2):
        d = jnp.int32(0)
        for k in range(LANES):
            d = d + jnp.where(upto[k] <= j, 1, 0)
        d = jnp.minimum(d, LANES - 1)
        settled[2 * j] = recv[2 * d]
        settled[2 * j + 1] = recv[2 * d + 1]
    project(settled, far_q)
    attend(far_q, far_done)
    settled[...] = far_t[...].T.reshape(CLUSTERS, CLUSTER, C)
    for d in range(LANES):
        held = back_recv if d == 0 else back_send
        j = jnp.minimum(upto[d] - active[d], LANES // 2 - 1)
        held[2 * d] = settled[2 * j]
        held[2 * d + 1] = settled[2 * j + 1]
    backs = []
    for d in range(1, LANES):
        copy = pltpu.make_async_remote_copy(
            src_ref=back_send.at[pl.ds(2 * d, 2)], dst_ref=back_recv.at[pl.ds(2 * d, 2)],
            send_sem=bout_sems.at[d], recv_sem=bin_sems.at[d], device_id=lane(-d), device_id_type=MESH,
        )
        copy.start()
        backs.append(copy)

    across.wait()
    set_keys(pool[:, :C])
    set_values(pool[:, C:].T)
    attend(near_q, merge)

    for copy in backs:
        copy.wait()
    for c in range(CLUSTERS):
        rank = jnp.int32(0)
        for e in range(c):
            rank = rank + jnp.where(offsets[e] == offsets[c], 1, 0)
        settled[c] = back_recv[2 * offsets[c] + jnp.minimum(rank, 1)]

    def tail(i, _):
        rows = pl.ds(pl.multiple_of(i * ROW_CHUNK, ROW_CHUNK), ROW_CHUNK)
        near = near_t[:, rows].T
        far = settled[pl.ds(i * (ROW_CHUNK // CLUSTER), ROW_CHUNK // CLUSTER)].reshape(ROW_CHUNK, C)
        after = (
            x_ref[rows, :].astype(F32)
            + jnp.dot(near, wout[...], preferred_element_type=F32)
            + jnp.dot(far, wout[...], preferred_element_type=F32)
        ).astype(BF)
        mlp_in = norm_rows(after, gain_m[...])
        hidden = jax.nn.gelu(jnp.dot(mlp_in, wup[...], preferred_element_type=F32), approximate=True).astype(BF)
        out[rows, :] = (
            after.astype(F32) + jnp.dot(hidden, wdown[...], preferred_element_type=F32)
        ).astype(BF)
        return 0

    lax.fori_loop(0, ROWS // ROW_CHUNK, tail, 0)


def per_device(points, gain_attn, w_query_key, w_value, w_out, gain_mlp, w_up, w_down, cluster_dest):
    vmem = pl.BlockSpec(memory_space=pltpu.VMEM)
    clusters = pltpu.VMEM((CLUSTERS, CLUSTER, C), BF)
    slots = pltpu.VMEM((2 * LANES, CLUSTER, C), BF)
    turned = pltpu.VMEM((C, ROWS), BF)
    result = pl.pallas_call(
        kernel,
        out_shape=jax.ShapeDtypeStruct((ROWS, C), BF),
        in_specs=[pl.BlockSpec(memory_space=pltpu.SMEM)] + [vmem] * 8,
        out_specs=vmem,
        scratch_shapes=[
            clusters, clusters,
            turned, turned,
            pltpu.VMEM((HEADS, ROWS, HEAD), BF),
            pltpu.VMEM((HEADS, 48, ROWS), BF),
            pltpu.VMEM((ROWS, 2 * C), BF),
            pltpu.VMEM((2 * GROUP, ROWS, QB), F32),
            pltpu.VMEM((2 * GROUP, ROWS, QB), BF),
            pltpu.VMEM((2 * GROUP, 8, QB), F32),
            pltpu.VMEM((HEADS, 48, ROWS), F32),
            pltpu.VMEM((HEADS, 8, ROWS), F32),
            turned, turned,
            slots, slots, slots, slots,
        ]
        + [pltpu.SemaphoreType.DMA((LANES,))] * 4
        + [pltpu.SemaphoreType.DMA((CHIPS,))] * 2,
        compiler_params=pltpu.CompilerParams(
            collective_id=0, has_side_effects=True, vmem_limit_bytes=60 * 1024 * 1024
        ),
        name="block",
    )(
        cluster_dest.reshape(CLUSTERS), points.reshape(ROWS, C), gain_attn.reshape(1, C), w_query_key,
        w_value, w_out, gain_mlp.reshape(1, C), w_up, w_down,
    )
    return result.reshape(points.shape)


def solution(mesh):
    placed = (P("ball", "region", None, None),) + (P(),) * 7 + (P("ball", "region", None),)
    return jax.shard_map(
        per_device, mesh=mesh, in_specs=placed, out_specs=P("ball", "region", None, None), check_vma=False
    )
```

```python
import functools
import math

import jax
import jax.numpy as jnp
from jax import lax
from jax.experimental import pallas as pl
from jax.experimental.pallas import tpu as pltpu
from jax.sharding import PartitionSpec as P

MESH = pl.DeviceIdType.MESH
BF = jnp.bfloat16
F32 = jnp.float32
HEADS = 8
HEAD = 32
C = 256
ROWS = 1024
CLUSTER = 64
CLUSTERS = 16
LANES = 16
POOL = 16
POOLED = ROWS // POOL
CHIPS = 8
QB = 512
QBLOCKS = ROWS // QB
BLOCKS = HEADS * QBLOCKS
GROUP = 2
PIECE = 128
DEPTH = 256
PARTS = 4
PART = C // PARTS
ROW_CHUNK = 256
SCALE = math.log2(math.e) / math.sqrt(HEAD)


def norm_rows(x, gain):
    x = x.astype(F32)
    scale = lax.rsqrt(jnp.mean(x * x, axis=1, keepdims=True) + 1e-6)
    return (x * scale * gain).astype(BF)


def kernel(
    dest, gain_a, gain_m, x_in, wqk_in, wv_in, wout_in, wup_in, wdown_in, out,
    x_ref, wqk, wv, wout, wup, wdown,
    normed, settled, near_q, far_q, keys, vals, pool, score, weight, tops, near_sum, near_max, near_t, far_t,
    send, recv, back_send, back_recv,
    out_sems, in_sems, bout_sems, bin_sems, pout_sems, pin_sems, load_sems,
):
    me = lax.axis_index("ball")
    spot = lax.axis_index("region")
    chip, core = spot // 2, spot % 2

    def lane(offset):
        return {"ball": lax.rem(me + offset + LANES, LANES)}

    def chip_at(offset):
        return {"region": lax.rem(chip + offset + CHIPS, CHIPS) * 2 + core}

    partner = {"region": chip * 2 + 1 - core}

    loads = [
        pltpu.make_async_copy(source, held, load_sems.at[k])
        for k, (source, held) in enumerate(
            ((x_in, x_ref), (wqk_in, wqk), (wv_in, wv), (wout_in, wout), (wup_in, wup), (wdown_in, wdown))
        )
    ]
    for load in loads:
        load.start()
    barrier = pltpu.get_barrier_semaphore()
    for d in range(1, LANES):
        pl.semaphore_signal(barrier, inc=1, device_id=lane(d), device_id_type=MESH)
    for d in range(1, CHIPS):
        pl.semaphore_signal(barrier, inc=1, device_id=chip_at(d), device_id_type=MESH)
    pl.semaphore_signal(barrier, inc=1, device_id=partner, device_id_type=MESH)

    offsets = [lax.bitwise_and(lax.shift_right_arithmetic(dest[c], 4) - me, LANES - 1) for c in range(CLUSTERS)]
    first, second, active, upto = [], [], [], []
    count = jnp.int32(0)
    for d in range(LANES):
        lo, hi = jnp.int32(CLUSTERS), jnp.int32(0)
        for c in range(CLUSTERS):
            hi = jnp.where(offsets[c] == d, c, hi)
            lo = jnp.where(offsets[CLUSTERS - 1 - c] == d, CLUSTERS - 1 - c, lo)
        hit = jnp.where(lo < CLUSTERS, 1, 0)
        count = count + hit
        first.append(jnp.minimum(lo, CLUSTERS - 1))
        second.append(hi)
        active.append(hit)
        upto.append(count)

    loads[0].wait()

    def norm_chunk(i, _):
        n = norm_rows(x_ref[pl.ds(pl.multiple_of(i * ROW_CHUNK, ROW_CHUNK), ROW_CHUNK), :], gain_a[...])
        normed[pl.ds(i * (ROW_CHUNK // CLUSTER), ROW_CHUNK // CLUSTER)] = n.reshape(
            ROW_CHUNK // CLUSTER, CLUSTER, C
        )
        return 0

    lax.fori_loop(0, ROWS // ROW_CHUNK, norm_chunk, 0)
    for d in range(LANES):
        held = recv if d == 0 else send
        held[2 * d] = normed[first[d]]
        held[2 * d + 1] = normed[second[d]]

    pl.semaphore_wait(barrier, LANES - 1 + CHIPS - 1 + 1)
    sends = []
    for d in range(1, LANES):
        copy = pltpu.make_async_remote_copy(
            src_ref=send.at[pl.ds(2 * d, 2)], dst_ref=recv.at[pl.ds(2 * d, 2)],
            send_sem=out_sems.at[d], recv_sem=in_sems.at[d], device_id=lane(d), device_id_type=MESH,
        )
        copy.start()
        sends.append(copy)

    def set_keys(rows):
        for h in range(HEADS):
            keys[h] = rows[:, h * HEAD:(h + 1) * HEAD]

    def set_values(value_t):
        for h in range(HEADS):
            vals[h, :HEAD, :] = value_t[h * HEAD:(h + 1) * HEAD, :]

    def project(source, query_t):
        states = source[...].reshape(ROWS, C)
        turned = states.T
        query_t[...] = jnp.dot(wqk[:, :C].T, turned, preferred_element_type=F32).astype(BF)
        key_rows = jnp.dot(states, wqk[:, C:], preferred_element_type=F32).astype(BF)
        set_keys(key_rows)
        set_values(jnp.dot(wv[...].T, turned, preferred_element_type=F32).astype(BF))
        return key_rows

    for h in range(HEADS):
        vals[h, HEAD:, :] = jnp.ones((16, ROWS), BF)
    for load in loads[1:3]:
        load.wait()
    key_rows = project(normed, near_q)

    row = lax.broadcasted_iota(jnp.int32, (POOLED, ROWS), 0)
    col = lax.broadcasted_iota(jnp.int32, (POOLED, ROWS), 1)
    pooling = jnp.where(col // POOL == row, 1.0 / math.sqrt(POOL), 0.0).astype(BF)
    pool[:POOLED, :C] = jnp.dot(pooling, key_rows, preferred_element_type=F32).astype(BF)
    value_rows = jnp.dot(normed[...].reshape(ROWS, C), wv[...], preferred_element_type=F32).astype(BF)
    pool[:POOLED, C:] = jnp.dot(pooling, value_rows, preferred_element_type=F32).astype(BF)
    pooled_sends = []
    for d in range(1, CHIPS):
        copy = pltpu.make_async_remote_copy(
            src_ref=pool.at[pl.ds(0, POOLED)], dst_ref=pool.at[pl.ds(d * POOLED, POOLED)],
            send_sem=pout_sems.at[d], recv_sem=pin_sems.at[d], device_id=chip_at(d), device_id_type=MESH,
        )
        copy.start()
        pooled_sends.append(copy)

    def attend(query_t, finish, between=None):
        def spot_of(i):
            return i // QBLOCKS, pl.ds(pl.multiple_of(i % QBLOCKS * QB, QB), QB)

        def head_rows(h):
            return pl.ds(pl.multiple_of(h * HEAD, HEAD), HEAD)

        def scores_of(i, slot, r, top):
            h, cols = spot_of(i)
            rows = pl.ds(r * PIECE, PIECE)
            s = jnp.dot(keys[h, rows, :], query_t[head_rows(h), cols], preferred_element_type=F32)
            score[slot, rows, :] = s
            for j in range(PIECE // 8):
                top = jnp.maximum(top, s[j * 8:(j + 1) * 8])
            return top

        def sum_of(h, slot, c, total):
            rows = pl.ds(c * DEPTH, DEPTH)
            return total + jnp.dot(vals[h, :, rows], weight[slot, rows, :], preferred_element_type=F32)

        def top_of(slot):
            return jnp.max(tops[slot], axis=0, keepdims=True)

        low = jnp.full((8, QB), -jnp.inf, F32)
        none = jnp.zeros((48, QB), F32)

        def step(g, even, last=False):
            for b in range(GROUP):
                i = g * GROUP + b
                now = b if even else GROUP + b
                other = GROUP + b if even else b
                old = jnp.maximum(i - GROUP, 0)
                new = jnp.minimum(i + GROUP, BLOCKS - 1)
                old_head, old_cols = spot_of(old)
                head, cols = spot_of(i)
                old_top = top_of(other)
                top = top_of(now)
                new_top, total, last_total = low, none, none
                for r in range(ROWS // PIECE):
                    rows = pl.ds(r * PIECE, PIECE)
                    if not last:
                        new_top = scores_of(new, other, r, new_top)
                    weight[now, rows, :] = jnp.exp2((score[now, rows, :] - top) * SCALE).astype(BF)
                    if (r + 1) * PIECE % DEPTH == 0:
                        part = (r + 1) * PIECE // DEPTH - 1
                        total = sum_of(old_head, other, part, total)
                        if last:
                            last_total = sum_of(head, now, part, last_total)
                finish(old_head, old_cols, old_top, total)
                if last:
                    finish(head, cols, top, last_total)
                else:
                    tops[other] = new_top

        for b in range(GROUP):
            top = low
            for r in range(ROWS // PIECE):
                top = scores_of(b, b, r, top)
            tops[b] = top

        pairs = BLOCKS // GROUP // 2

        def pair(t, _):
            @pl.when(t < pairs)
            def _():
                step(2 * t, True)

            if between is not None:
                @pl.when(t >= 1)
                def _():
                    between(t - 1)

            @pl.when(t < pairs - 1)
            def _():
                step(2 * t + 1, False)

            @pl.when(t == pairs - 1)
            def _():
                step(2 * t + 1, False, last=True)

            return 0

        lax.fori_loop(0, pairs, pair, 0)

    def keep(h, cols, top, total):
        near_sum[h, :, cols] = total
        near_max[h, :, cols] = jnp.broadcast_to(top, (8, QB))

    def head_rows(h):
        return pl.ds(pl.multiple_of(h * HEAD, HEAD), HEAD)

    def close(total):
        return (total[:HEAD] / total[HEAD:HEAD + 1]).astype(BF)

    def merge(h, cols, top, total):
        before = near_max[h, :1, cols]
        both = jnp.maximum(before, top)
        whole = near_sum[h, :, cols] * jnp.exp2((before - both) * SCALE) + total * jnp.exp2((top - both) * SCALE)
        near_t[head_rows(h), cols] = close(whole)

    def far_done(h, cols, top, total):
        rows = pl.ds(pl.multiple_of(h % 2 * HEAD, HEAD), HEAD)
        block = close(total)
        for k in range(QB // (2 * CLUSTER)):
            at = h // 2 * (LANES // 2) + cols.start // (2 * CLUSTER) + k
            far_t[at, rows, :] = block[:, k * 2 * CLUSTER:(k + 1) * 2 * CLUSTER]

    attend(near_q, keep)

    for copy in pooled_sends:
        copy.wait()
    across = pltpu.make_async_remote_copy(
        src_ref=pool.at[pl.ds(0, ROWS // 2)], dst_ref=pool.at[pl.ds(ROWS // 2, ROWS // 2)],
        send_sem=pout_sems.at[0], recv_sem=pin_sems.at[0], device_id=partner, device_id_type=MESH,
    )
    across.start()

    for copy in sends:
        copy.wait()
    picks = []
    for j in range(LANES // 2):
        d = jnp.int32(0)
        for k in range(LANES):
            d = d + jnp.where(upto[k] <= j, 1, 0)
        d = jnp.minimum(d, LANES - 1)
        picks.append(d)
        settled[2 * j] = recv[2 * d]
        settled[2 * j + 1] = recv[2 * d + 1]
    project(settled, far_q)
    def back_copy(part, d):
        at = part * LANES + d
        return pltpu.make_async_remote_copy(
            src_ref=back_send.at[at], dst_ref=back_recv.at[at],
            send_sem=bout_sems.at[at], recv_sem=bin_sems.at[at], device_id=lane(-d), device_id_type=MESH,
        )

    def send_back(part):
        for d in range(LANES):
            held = back_recv if d == 0 else back_send
            j = jnp.minimum(upto[d] - active[d], LANES // 2 - 1)
            held[part * LANES + d] = far_t[part * (LANES // 2) + j]
        for d in range(1, LANES):
            back_copy(part, d).start()

    attend(far_q, far_done, send_back)
    send_back(PARTS - 1)

    across.wait()
    set_keys(pool[:, :C])
    set_values(pool[:, C:].T)
    attend(near_q, merge)

    for part in range(PARTS):
        for d in range(1, LANES):
            back_copy(part, d).wait()
    for j in range(LANES // 2):
        block = jnp.concatenate([back_recv[part * LANES + picks[j]] for part in range(PARTS)], axis=0)
        normed[2 * j:2 * j + 2] = block.T.reshape(2, CLUSTER, C)
    for c in range(CLUSTERS):
        at = jnp.int32(0)
        for j in range(LANES // 2 - 1):
            at = at + jnp.where(picks[j] < offsets[c], 2, 0)
        rank = jnp.int32(0)
        for e in range(c):
            rank = rank + jnp.where(offsets[e] == offsets[c], 1, 0)
        settled[c] = normed[at + jnp.minimum(rank, 1)]
    for load in loads[3:]:
        load.wait()

    def tail(i, _):
        rows = pl.ds(pl.multiple_of(i * ROW_CHUNK, ROW_CHUNK), ROW_CHUNK)
        near = near_t[:, rows].T
        far = settled[pl.ds(i * (ROW_CHUNK // CLUSTER), ROW_CHUNK // CLUSTER)].reshape(ROW_CHUNK, C)
        after = (
            x_ref[rows, :].astype(F32)
            + jnp.dot(near, wout[...], preferred_element_type=F32)
            + jnp.dot(far, wout[...], preferred_element_type=F32)
        ).astype(BF)
        mlp_in = norm_rows(after, gain_m[...])
        hidden = jax.nn.gelu(jnp.dot(mlp_in, wup[...], preferred_element_type=F32), approximate=True).astype(BF)
        out[rows, :] = (
            after.astype(F32) + jnp.dot(hidden, wdown[...], preferred_element_type=F32)
        ).astype(BF)
        return 0

    lax.fori_loop(0, ROWS // ROW_CHUNK, tail, 0)


def per_device(points, gain_attn, w_query_key, w_value, w_out, gain_mlp, w_up, w_down, cluster_dest):
    vmem = pl.BlockSpec(memory_space=pltpu.VMEM)
    clusters = pltpu.VMEM((CLUSTERS, CLUSTER, C), BF)
    slots = pltpu.VMEM((2 * LANES, CLUSTER, C), BF)
    turned = pltpu.VMEM((C, ROWS), BF)
    parts = pltpu.VMEM((PARTS * LANES, PART, 2 * CLUSTER), BF)
    anywhere = pl.BlockSpec(memory_space=pl.ANY)
    moved = (points.reshape(ROWS, C), w_query_key, w_value, w_out, w_up, w_down)
    result = pl.pallas_call(
        kernel,
        out_shape=jax.ShapeDtypeStruct((ROWS, C), BF),
        in_specs=[pl.BlockSpec(memory_space=pltpu.SMEM)] + [vmem] * 2 + [anywhere] * 6,
        out_specs=vmem,
        scratch_shapes=[pltpu.VMEM(a.shape, BF) for a in moved]
        + [
            clusters, clusters,
            turned, turned,
            pltpu.VMEM((HEADS, ROWS, HEAD), BF),
            pltpu.VMEM((HEADS, 48, ROWS), BF),
            pltpu.VMEM((ROWS, 2 * C), BF),
            pltpu.VMEM((2 * GROUP, ROWS, QB), F32),
            pltpu.VMEM((2 * GROUP, ROWS, QB), BF),
            pltpu.VMEM((2 * GROUP, 8, QB), F32),
            pltpu.VMEM((HEADS, 48, ROWS), F32),
            pltpu.VMEM((HEADS, 8, ROWS), F32),
            turned,
            pltpu.VMEM((PARTS * LANES // 2, PART, 2 * CLUSTER), BF),
            slots, slots, parts, parts,
        ]
        + [pltpu.SemaphoreType.DMA((LANES,))] * 2
        + [pltpu.SemaphoreType.DMA((PARTS * LANES,))] * 2
        + [pltpu.SemaphoreType.DMA((CHIPS,))] * 3,
        compiler_params=pltpu.CompilerParams(
            collective_id=0, has_side_effects=True, vmem_limit_bytes=60 * 1024 * 1024
        ),
        name="block",
    )(
        cluster_dest.reshape(CLUSTERS), gain_attn.reshape(1, C), gain_mlp.reshape(1, C), *moved
    )
    return result.reshape(points.shape)


def solution(mesh):
    placed = (P("ball", "region", None, None),) + (P(),) * 7 + (P("ball", "region", None),)
    return jax.shard_map(
        per_device, mesh=mesh, in_specs=placed, out_specs=P("ball", "region", None, None), check_vma=False
    )
```

```python
import functools
import math

import jax
import jax.numpy as jnp
from jax import lax
from jax.experimental import pallas as pl
from jax.experimental.pallas import tpu as pltpu
from jax.sharding import PartitionSpec as P

MESH = pl.DeviceIdType.MESH
BF = jnp.bfloat16
F32 = jnp.float32
HEADS = 8
HEAD = 32
C = 256
ROWS = 1024
CLUSTER = 64
CLUSTERS = 16
LANES = 16
POOL = 16
POOLED = ROWS // POOL
CHIPS = 8
QB = 512
QBLOCKS = ROWS // QB
BLOCKS = HEADS * QBLOCKS
GROUP = 2
PIECE = 128
DEPTH = 256
PARTS = 4
PART = C // PARTS
HIDDEN = 1024
MLP_ROWS = 512
GELU_A = math.sqrt(2 / math.pi)
GELU_B = GELU_A * 0.044715
MLP_SPLIT = 4
ROW_CHUNK = 256
SCALE = math.log2(math.e) / math.sqrt(HEAD)


def norm_rows(x, gain):
    x = x.astype(F32)
    scale = lax.rsqrt(jnp.mean(x * x, axis=1, keepdims=True) + 1e-6)
    return (x * scale * gain).astype(BF)


def kernel(
    x_in, wqk_in, wv_in, wout_in, gain_in, dest_in, out,
    x_ref, wqk, wv, wout, gain_a, dest,
    normed, settled, near_q, far_q, keys, vals, pool, score, weight, tops, near_sum, near_max, near_t, far_t,
    send, recv, back_send, back_recv,
    out_sems, in_sems, bout_sems, bin_sems, pout_sems, pin_sems, load_sems,
):
    me = lax.axis_index("ball")
    spot = lax.axis_index("region")
    chip, core = spot // 2, spot % 2

    def lane(offset):
        return {"ball": lax.rem(me + offset + LANES, LANES)}

    def chip_at(offset):
        return {"region": lax.rem(chip + offset + CHIPS, CHIPS) * 2 + core}

    partner = {"region": chip * 2 + 1 - core}

    loads = [
        pltpu.make_async_copy(source, held, load_sems.at[k])
        for k, (source, held) in enumerate(
            ((x_in, x_ref), (wqk_in, wqk), (wv_in, wv), (wout_in, wout), (gain_in, gain_a), (dest_in, dest))
        )
    ]
    for load in loads[::-1]:
        load.start()
    barrier = pltpu.get_barrier_semaphore()
    for d in range(1, LANES):
        pl.semaphore_signal(barrier, inc=1, device_id=lane(d), device_id_type=MESH)
    for d in range(1, CHIPS):
        pl.semaphore_signal(barrier, inc=1, device_id=chip_at(d), device_id_type=MESH)
    pl.semaphore_signal(barrier, inc=1, device_id=partner, device_id_type=MESH)

    loads[5].wait()
    offsets = [lax.bitwise_and(lax.shift_right_arithmetic(dest[c], 4) - me, LANES - 1) for c in range(CLUSTERS)]
    first, second, active, upto = [], [], [], []
    count = jnp.int32(0)
    for d in range(LANES):
        lo, hi = jnp.int32(CLUSTERS), jnp.int32(0)
        for c in range(CLUSTERS):
            hi = jnp.where(offsets[c] == d, c, hi)
            lo = jnp.where(offsets[CLUSTERS - 1 - c] == d, CLUSTERS - 1 - c, lo)
        hit = jnp.where(lo < CLUSTERS, 1, 0)
        count = count + hit
        first.append(jnp.minimum(lo, CLUSTERS - 1))
        second.append(hi)
        active.append(hit)
        upto.append(count)

    loads[4].wait()
    loads[0].wait()

    for c in range(CLUSTERS):
        normed[c] = norm_rows(x_ref[c * CLUSTER:(c + 1) * CLUSTER, :], gain_a[...])
    for d in range(LANES):
        held = recv if d == 0 else send
        held[2 * d] = normed[first[d]]
        held[2 * d + 1] = normed[second[d]]

    pl.semaphore_wait(barrier, LANES - 1 + CHIPS - 1 + 1)
    for d in range(1, LANES):
        copy = pltpu.make_async_remote_copy(
            src_ref=send.at[pl.ds(2 * d, 2)], dst_ref=recv.at[pl.ds(2 * d, 2)],
            send_sem=out_sems.at[0], recv_sem=in_sems.at[0], device_id=lane(d), device_id_type=MESH,
        )
        copy.start()

    def set_keys(rows):
        for h in range(HEADS):
            keys[h] = rows[:, h * HEAD:(h + 1) * HEAD]

    def set_values(value_t):
        for h in range(HEADS):
            vals[h, :HEAD, :] = value_t[h * HEAD:(h + 1) * HEAD, :]

    def project(source, query_t):
        states = source[...].reshape(ROWS, C)
        turned = states.T
        query_t[...] = jnp.dot(wqk[:, :C].T, turned, preferred_element_type=F32).astype(BF)
        key_rows = jnp.dot(states, wqk[:, C:], preferred_element_type=F32).astype(BF)
        set_keys(key_rows)
        set_values(jnp.dot(wv[...].T, turned, preferred_element_type=F32).astype(BF))
        return key_rows

    for h in range(HEADS):
        vals[h, HEAD:, :] = jnp.ones((16, ROWS), BF)
    for load in loads[1:3]:
        load.wait()
    key_rows = project(normed, near_q)

    row = lax.broadcasted_iota(jnp.int32, (POOLED, ROWS), 0)
    col = lax.broadcasted_iota(jnp.int32, (POOLED, ROWS), 1)
    pooling = jnp.where(col // POOL == row, 1.0 / math.sqrt(POOL), 0.0).astype(BF)
    pool[:POOLED, :C] = jnp.dot(pooling, key_rows, preferred_element_type=F32).astype(BF)
    value_rows = jnp.dot(normed[...].reshape(ROWS, C), wv[...], preferred_element_type=F32).astype(BF)
    pool[:POOLED, C:] = jnp.dot(pooling, value_rows, preferred_element_type=F32).astype(BF)
    for d in range(1, CHIPS):
        copy = pltpu.make_async_remote_copy(
            src_ref=pool.at[pl.ds(0, POOLED)], dst_ref=pool.at[pl.ds(d * POOLED, POOLED)],
            send_sem=pout_sems.at[1], recv_sem=pin_sems.at[1], device_id=chip_at(d), device_id_type=MESH,
        )
        copy.start()

    def attend(query_t, finish, between=None):
        def spot_of(i):
            return i // QBLOCKS, pl.ds(pl.multiple_of(i % QBLOCKS * QB, QB), QB)

        def head_rows(h):
            return pl.ds(pl.multiple_of(h * HEAD, HEAD), HEAD)

        def scores_of(i, slot, r, top):
            h, cols = spot_of(i)
            rows = pl.ds(r * PIECE, PIECE)
            s = jnp.dot(keys[h, rows, :], query_t[head_rows(h), cols], preferred_element_type=F32)
            score[slot, rows, :] = s
            for j in range(PIECE // 8):
                top = jnp.maximum(top, s[j * 8:(j + 1) * 8])
            return top

        def sum_of(h, slot, c, total):
            rows = pl.ds(c * DEPTH, DEPTH)
            return total + jnp.dot(vals[h, :, rows], weight[slot, rows, :], preferred_element_type=F32)

        def top_of(slot):
            return jnp.max(tops[slot], axis=0, keepdims=True)

        low = jnp.full((8, QB), -jnp.inf, F32)
        none = jnp.zeros((48, QB), F32)

        def step(g, even, last=False):
            for b in range(GROUP):
                i = g * GROUP + b
                now = b if even else GROUP + b
                other = GROUP + b if even else b
                old = jnp.maximum(i - GROUP, 0)
                new = jnp.minimum(i + GROUP, BLOCKS - 1)
                old_head, old_cols = spot_of(old)
                head, cols = spot_of(i)
                old_top = top_of(other)
                top = top_of(now)
                new_top, total, last_total = low, none, none
                for r in range(ROWS // PIECE):
                    rows = pl.ds(r * PIECE, PIECE)
                    if not last:
                        new_top = scores_of(new, other, r, new_top)
                    weight[now, rows, :] = jnp.exp2((score[now, rows, :] - top) * SCALE).astype(BF)
                    if (r + 1) * PIECE % DEPTH == 0:
                        part = (r + 1) * PIECE // DEPTH - 1
                        total = sum_of(old_head, other, part, total)
                        if last:
                            last_total = sum_of(head, now, part, last_total)
                finish(old_head, old_cols, old_top, total)
                if last:
                    finish(head, cols, top, last_total)
                else:
                    tops[other] = new_top

        for b in range(GROUP):
            top = low
            for r in range(ROWS // PIECE):
                top = scores_of(b, b, r, top)
            tops[b] = top

        pairs = BLOCKS // GROUP // 2

        def pair(t, _):
            @pl.when(t < pairs)
            def _():
                step(2 * t, True)

            if between is not None:
                @pl.when(t >= 1)
                def _():
                    between(t - 1)

            @pl.when(t < pairs - 1)
            def _():
                step(2 * t + 1, False)

            @pl.when(t == pairs - 1)
            def _():
                step(2 * t + 1, False, last=True)

            return 0

        lax.fori_loop(0, pairs, pair, 0)

    def keep(h, cols, top, total):
        near_sum[h, :, cols] = total
        near_max[h, :, cols] = jnp.broadcast_to(top, (8, QB))

    def head_rows(h):
        return pl.ds(pl.multiple_of(h * HEAD, HEAD), HEAD)

    def close(total):
        return (total[:HEAD] / total[HEAD:HEAD + 1]).astype(BF)

    def merge(h, cols, top, total):
        before = near_max[h, :1, cols]
        both = jnp.maximum(before, top)
        whole = near_sum[h, :, cols] * jnp.exp2((before - both) * SCALE) + total * jnp.exp2((top - both) * SCALE)
        near_t[head_rows(h), cols] = close(whole)

    def far_done(h, cols, top, total):
        rows = pl.ds(pl.multiple_of(h % 2 * HEAD, HEAD), HEAD)
        block = close(total)
        for k in range(QB // (2 * CLUSTER)):
            at = h // 2 * (LANES // 2) + cols.start // (2 * CLUSTER) + k
            far_t[at, rows, :] = block[:, k * 2 * CLUSTER:(k + 1) * 2 * CLUSTER]

    attend(near_q, keep)

    pltpu.make_async_remote_copy(
        src_ref=pool.at[pl.ds(POOLED, ROWS // 2 - POOLED)], dst_ref=pool.at[pl.ds(POOLED, ROWS // 2 - POOLED)],
        send_sem=pout_sems.at[1], recv_sem=pin_sems.at[1], device_id=chip_at(1), device_id_type=MESH,
    ).wait()
    across = pltpu.make_async_remote_copy(
        src_ref=pool.at[pl.ds(0, ROWS // 2)], dst_ref=pool.at[pl.ds(ROWS // 2, ROWS // 2)],
        send_sem=pout_sems.at[0], recv_sem=pin_sems.at[0], device_id=partner, device_id_type=MESH,
    )
    across.start()

    pltpu.make_async_remote_copy(
        src_ref=send.at[pl.ds(2, 2 * LANES - 2)], dst_ref=recv.at[pl.ds(2, 2 * LANES - 2)],
        send_sem=out_sems.at[0], recv_sem=in_sems.at[0], device_id=lane(1), device_id_type=MESH,
    ).wait()
    picks = []
    for j in range(LANES // 2):
        d = jnp.int32(0)
        for k in range(LANES):
            d = d + jnp.where(upto[k] <= j, 1, 0)
        d = jnp.minimum(d, LANES - 1)
        picks.append(d)
        settled[2 * j] = recv[2 * d]
        settled[2 * j + 1] = recv[2 * d + 1]
    project(settled, far_q)
    def back_copy(part, d):
        at = part * LANES + d
        return pltpu.make_async_remote_copy(
            src_ref=back_send.at[at], dst_ref=back_recv.at[at],
            send_sem=bout_sems.at[part], recv_sem=bin_sems.at[part], device_id=lane(-d), device_id_type=MESH,
        )

    def send_back(part):
        for d in range(LANES):
            held = back_recv if d == 0 else back_send
            j = jnp.minimum(upto[d] - active[d], LANES // 2 - 1)
            held[part * LANES + d] = far_t[part * (LANES // 2) + j]
        for d in range(1, LANES):
            back_copy(part, d).start()

    attend(far_q, far_done, send_back)
    send_back(PARTS - 1)

    across.wait()
    set_keys(pool[:, :C])
    set_values(pool[:, C:].T)
    attend(near_q, merge)

    for part in range(PARTS):
        rest = pl.ds(part * LANES + 1, LANES - 1)
        pltpu.make_async_remote_copy(
            src_ref=back_send.at[rest], dst_ref=back_recv.at[rest],
            send_sem=bout_sems.at[part], recv_sem=bin_sems.at[part], device_id=lane(1), device_id_type=MESH,
        ).wait()
    for j in range(LANES // 2):
        block = jnp.concatenate([back_recv[part * LANES + picks[j]] for part in range(PARTS)], axis=0)
        normed[2 * j:2 * j + 2] = block.T.reshape(2, CLUSTER, C)
    for c in range(CLUSTERS):
        at = jnp.int32(0)
        for j in range(LANES // 2 - 1):
            at = at + jnp.where(picks[j] < offsets[c], 2, 0)
        rank = jnp.int32(0)
        for e in range(c):
            rank = rank + jnp.where(offsets[e] == offsets[c], 1, 0)
        settled[c] = normed[at + jnp.minimum(rank, 1)]
    loads[3].wait()

    def tail(i, _):
        rows = pl.ds(pl.multiple_of(i * ROW_CHUNK, ROW_CHUNK), ROW_CHUNK)
        near = near_t[:, rows].T
        far = settled[pl.ds(i * (ROW_CHUNK // CLUSTER), ROW_CHUNK // CLUSTER)].reshape(ROW_CHUNK, C)
        out[rows, :] = (
            x_ref[rows, :].astype(F32)
            + jnp.dot(near, wout[...], preferred_element_type=F32)
            + jnp.dot(far, wout[...], preferred_element_type=F32)
        ).astype(BF)
        return 0

    lax.fori_loop(0, ROWS // ROW_CHUNK, tail, 0)


def gelu(x):
    half = 0.5 * x
    inner = x * (GELU_A + GELU_B * (x * x))
    return half + half * jnp.tanh(inner)


def mlp_kernel(after_ref, gain_m, wup, wdown, out):
    after = after_ref[...]
    mlp_in = norm_rows(after, gain_m[...])
    total = after.astype(F32)
    for k in range(MLP_SPLIT):
        cols = pl.ds(k * (HIDDEN // MLP_SPLIT), HIDDEN // MLP_SPLIT)
        hidden = gelu(jnp.dot(mlp_in, wup[:, cols], preferred_element_type=F32)).astype(BF)
        total = total + jnp.dot(hidden, wdown[cols, :], preferred_element_type=F32)
    out[...] = total.astype(BF)


def per_device(points, gain_attn, w_query_key, w_value, w_out, gain_mlp, w_up, w_down, cluster_dest):
    vmem = pl.BlockSpec(memory_space=pltpu.VMEM)
    clusters = pltpu.VMEM((CLUSTERS, CLUSTER, C), BF)
    slots = pltpu.VMEM((2 * LANES, CLUSTER, C), BF)
    turned = pltpu.VMEM((C, ROWS), BF)
    parts = pltpu.VMEM((PARTS * LANES, PART, 2 * CLUSTER), BF)
    anywhere = pl.BlockSpec(memory_space=pltpu.HBM)
    moved = (points.reshape(ROWS, C), w_query_key, w_value, w_out, gain_attn.reshape(1, C), cluster_dest.reshape(CLUSTERS))
    moved = tuple(pltpu.with_memory_space_constraint(a, pltpu.HBM) for a in moved)
    after = pl.pallas_call(
        kernel,
        out_shape=jax.ShapeDtypeStruct((ROWS, C), BF),
        in_specs=[anywhere] * 6,
        out_specs=vmem,
        scratch_shapes=[pltpu.VMEM(a.shape, a.dtype) for a in moved[:-1]]
        + [pltpu.SMEM((CLUSTERS,), jnp.int32)]
        + [
            clusters, clusters,
            turned, turned,
            pltpu.VMEM((HEADS, ROWS, HEAD), BF),
            pltpu.VMEM((HEADS, 48, ROWS), BF),
            pltpu.VMEM((ROWS, 2 * C), BF),
            pltpu.VMEM((2 * GROUP, ROWS, QB), F32),
            pltpu.VMEM((2 * GROUP, ROWS, QB), BF),
            pltpu.VMEM((2 * GROUP, 8, QB), F32),
            pltpu.VMEM((HEADS, 48, ROWS), F32),
            pltpu.VMEM((HEADS, 8, ROWS), F32),
            turned,
            pltpu.VMEM((PARTS * LANES // 2, PART, 2 * CLUSTER), BF),
            slots, slots, parts, parts,
        ]
        + [pltpu.SemaphoreType.DMA((1,))] * 2
        + [pltpu.SemaphoreType.DMA((PARTS,))] * 2
        + [pltpu.SemaphoreType.DMA((2,))] * 2
        + [pltpu.SemaphoreType.DMA((6,))],
        compiler_params=pltpu.CompilerParams(
            collective_id=0, has_side_effects=True, vmem_limit_bytes=40 * 1024 * 1024
        ),
        name="block",
    )(
        *moved
    )
    rows = pl.BlockSpec((MLP_ROWS, C), lambda i: (i, 0))
    result = pl.pallas_call(
        mlp_kernel,
        grid=(ROWS // MLP_ROWS,),
        out_shape=jax.ShapeDtypeStruct((ROWS, C), BF),
        in_specs=[rows] + [vmem] * 3,
        out_specs=rows,
        compiler_params=pltpu.CompilerParams(vmem_limit_bytes=12 * 1024 * 1024),
        name="mlp",
    )(after, gain_mlp.reshape(1, C), w_up, w_down)
    return result.reshape(points.shape)


def solution(mesh):
    placed = (P("ball", "region", None, None),) + (P(),) * 7 + (P("ball", "region", None),)
    return jax.shard_map(
        per_device, mesh=mesh, in_specs=placed, out_specs=P("ball", "region", None, None), check_vma=False
    )
```

```python
import functools
import math

import jax
import jax.numpy as jnp
from jax import lax
from jax.experimental import pallas as pl
from jax.experimental.pallas import tpu as pltpu
from jax.sharding import PartitionSpec as P

MESH = pl.DeviceIdType.MESH
BF = jnp.bfloat16
F32 = jnp.float32
HEADS = 8
HEAD = 32
C = 256
ROWS = 1024
CLUSTER = 64
CLUSTERS = 16
LANES = 16
POOL = 16
POOLED = ROWS // POOL
CHIPS = 8
QB = 512
QBLOCKS = ROWS // QB
BLOCKS = HEADS * QBLOCKS
GROUP = 2
PIECE = 128
DEPTH = 256
PARTS = 4
PART = C // PARTS
HIDDEN = 1024
MLP_ROWS = 512
GELU_A = math.sqrt(2 / math.pi)
GELU_B = GELU_A * 0.044715
MLP_SPLIT = 4
ROW_CHUNK = 256
SCALE = math.log2(math.e) / math.sqrt(HEAD)


def norm_rows(x, gain):
    x = x.astype(F32)
    scale = lax.rsqrt(jnp.mean(x * x, axis=1, keepdims=True) + 1e-6)
    return (x * scale * gain).astype(BF)


def kernel(
    x_in, wqk_in, wv_in, wout_in, gain_in, dest_in, out,
    x_ref, wqk, wv, wout, gain_a, dest,
    normed, settled, near_q, far_q, keys, vals, pool_keys, pool_vals, pool, score, weight, tops, near_sum, near_max, near_t, far_t,
    send, recv, back_send, back_recv,
    out_sems, in_sems, bout_sems, bin_sems, pout_sems, pin_sems, load_sems,
):
    me = lax.axis_index("ball")
    spot = lax.axis_index("region")
    chip, core = spot // 2, spot % 2

    def lane(offset):
        return {"ball": lax.rem(me + offset + LANES, LANES)}

    def chip_at(offset):
        return {"region": lax.rem(chip + offset + CHIPS, CHIPS) * 2 + core}

    partner = {"region": chip * 2 + 1 - core}

    loads = [
        pltpu.make_async_copy(source, held, load_sems.at[k])
        for k, (source, held) in enumerate(
            ((x_in, x_ref), (wqk_in, wqk), (wv_in, wv), (wout_in, wout), (gain_in, gain_a), (dest_in, dest))
        )
    ]
    for load in loads[::-1]:
        load.start()
    barrier = pltpu.get_barrier_semaphore()
    for d in range(1, LANES):
        pl.semaphore_signal(barrier, inc=1, device_id=lane(d), device_id_type=MESH)
    for d in range(1, CHIPS):
        pl.semaphore_signal(barrier, inc=1, device_id=chip_at(d), device_id_type=MESH)
    pl.semaphore_signal(barrier, inc=1, device_id=partner, device_id_type=MESH)

    loads[5].wait()
    offsets = [lax.bitwise_and(lax.shift_right_arithmetic(dest[c], 4) - me, LANES - 1) for c in range(CLUSTERS)]
    first, second, active, upto = [], [], [], []
    count = jnp.int32(0)
    for d in range(LANES):
        lo, hi = jnp.int32(CLUSTERS), jnp.int32(0)
        for c in range(CLUSTERS):
            hi = jnp.where(offsets[c] == d, c, hi)
            lo = jnp.where(offsets[CLUSTERS - 1 - c] == d, CLUSTERS - 1 - c, lo)
        hit = jnp.where(lo < CLUSTERS, 1, 0)
        count = count + hit
        first.append(jnp.minimum(lo, CLUSTERS - 1))
        second.append(hi)
        active.append(hit)
        upto.append(count)

    loads[4].wait()
    loads[0].wait()

    for c in range(CLUSTERS):
        normed[c] = norm_rows(x_ref[c * CLUSTER:(c + 1) * CLUSTER, :], gain_a[...])
    for d in range(LANES):
        held = recv if d == 0 else send
        held[2 * d] = normed[first[d]]
        held[2 * d + 1] = normed[second[d]]

    pl.semaphore_wait(barrier, LANES - 1 + CHIPS - 1 + 1)
    for d in range(1, LANES):
        copy = pltpu.make_async_remote_copy(
            src_ref=send.at[pl.ds(2 * d, 2)], dst_ref=recv.at[pl.ds(2 * d, 2)],
            send_sem=out_sems.at[0], recv_sem=in_sems.at[0], device_id=lane(d), device_id_type=MESH,
        )
        copy.start()

    def head_cols(rows, h):
        start = h % 4 * HEAD
        half = rows[:, h // 4 * 128:(h // 4 + 1) * 128]
        return (pltpu.roll(half, 128 - start, axis=1) if start else half)[:, :HEAD]

    def set_keys(rows):
        for h in range(HEADS):
            keys[h] = head_cols(rows, h)

    def set_values(held, value_t, first_head=0):
        for h in range(value_t.shape[0] // HEAD):
            held[first_head + h, :HEAD, :] = value_t[h * HEAD:(h + 1) * HEAD, :]

    def project(source, query_t):
        states = source[...].reshape(ROWS, C)
        turned = states.T
        query_t[...] = jnp.dot(wqk[:, :C].T, turned, preferred_element_type=F32).astype(BF)
        key_rows = jnp.dot(states, wqk[:, C:], preferred_element_type=F32).astype(BF)
        set_keys(key_rows)
        set_values(vals, jnp.dot(wv[...].T, turned, preferred_element_type=F32).astype(BF))
        return key_rows

    for h in range(HEADS):
        vals[h, HEAD:, :] = jnp.ones((16, ROWS), BF)
        pool_vals[h, HEAD:, :] = jnp.ones((16, ROWS), BF)
    for load in loads[1:3]:
        load.wait()
    key_rows = project(normed, near_q)

    row = lax.broadcasted_iota(jnp.int32, (POOLED, ROWS), 0)
    col = lax.broadcasted_iota(jnp.int32, (POOLED, ROWS), 1)
    pooling = jnp.where(col // POOL == row, 1.0 / math.sqrt(POOL), 0.0).astype(BF)
    pool[:POOLED, :C] = jnp.dot(pooling, key_rows, preferred_element_type=F32).astype(BF)
    value_rows = jnp.dot(normed[...].reshape(ROWS, C), wv[...], preferred_element_type=F32).astype(BF)
    pool[:POOLED, C:] = jnp.dot(pooling, value_rows, preferred_element_type=F32).astype(BF)
    for d in range(1, CHIPS):
        copy = pltpu.make_async_remote_copy(
            src_ref=pool.at[pl.ds(0, POOLED)], dst_ref=pool.at[pl.ds(d * POOLED, POOLED)],
            send_sem=pout_sems.at[1], recv_sem=pin_sems.at[1], device_id=chip_at(d), device_id_type=MESH,
        )
        copy.start()

    def attend(query_t, keys, vals, finish, between=None, ready=False, following=None, before_last=None, side=None):
        def spot_of(i):
            return i // QBLOCKS, pl.ds(pl.multiple_of(i % QBLOCKS * QB, QB), QB)

        def head_rows(h):
            return pl.ds(pl.multiple_of(h * HEAD, HEAD), HEAD)

        def scores_of(i, slot, r, top, query_t=query_t, keys=keys):
            h, cols = spot_of(i)
            rows = pl.ds(r * PIECE, PIECE)
            s = jnp.dot(keys[h, rows, :], query_t[head_rows(h), cols], preferred_element_type=F32)
            score[slot, rows, :] = s
            for j in range(PIECE // 8):
                top = jnp.maximum(top, s[j * 8:(j + 1) * 8])
            return top

        def sum_of(h, slot, c, total):
            rows = pl.ds(c * DEPTH, DEPTH)
            return total + jnp.dot(vals[h, :, rows], weight[slot, rows, :], preferred_element_type=F32)

        def top_of(slot):
            return jnp.max(tops[slot], axis=0, keepdims=True)

        low = jnp.full((8, QB), -jnp.inf, F32)
        none = jnp.zeros((48, QB), F32)

        def step(g, even, last=False):
            for b in range(GROUP):
                i = g * GROUP + b
                now = b if even else GROUP + b
                other = GROUP + b if even else b
                old = jnp.maximum(i - GROUP, 0)
                new = jnp.minimum(i + GROUP, BLOCKS - 1)
                old_head, old_cols = spot_of(old)
                head, cols = spot_of(i)
                old_top = top_of(other)
                top = top_of(now)
                new_top, total, last_total = low, none, none
                for r in range(ROWS // PIECE):
                    rows = pl.ds(r * PIECE, PIECE)
                    if not last:
                        new_top = scores_of(new, other, r, new_top)
                    else:
                        if side is not None:
                            side(b * (ROWS // PIECE) + r)
                        if following is not None:
                            new_top = scores_of(b, other, r, new_top, *following)
                    weight[now, rows, :] = jnp.exp2((score[now, rows, :] - top) * SCALE).astype(BF)
                    if (r + 1) * PIECE % DEPTH == 0:
                        part = (r + 1) * PIECE // DEPTH - 1
                        total = sum_of(old_head, other, part, total)
                        if last:
                            last_total = sum_of(head, now, part, last_total)
                finish(old_head, old_cols, old_top, total)
                if last:
                    finish(head, cols, top, last_total)
                if not last or following is not None:
                    tops[other] = new_top

        for b in range(0 if ready else GROUP):
            top = low
            for r in range(ROWS // PIECE):
                top = scores_of(b, b, r, top)
            tops[b] = top

        pairs = BLOCKS // GROUP // 2

        def pair(t, _):
            @pl.when(t < pairs)
            def _():
                step(2 * t, True)

            if between is not None:
                @pl.when(t >= 1)
                def _():
                    between(t - 1)

            @pl.when(t < pairs - 1)
            def _():
                step(2 * t + 1, False)

            if before_last is not None:
                pl.when(t == pairs - 1)(before_last)

            @pl.when(t == pairs - 1)
            def _():
                step(2 * t + 1, False, last=True)

            return 0

        lax.fori_loop(0, pairs, pair, 0)

    def keep(h, cols, top, total):
        near_sum[h, :, cols] = total
        near_max[h, :, cols] = jnp.broadcast_to(top, (8, QB))

    def head_rows(h):
        return pl.ds(pl.multiple_of(h * HEAD, HEAD), HEAD)

    def close(total):
        return (total[:HEAD] / total[HEAD:HEAD + 1]).astype(BF)

    def merge(h, cols, top, total):
        before = near_max[h, :1, cols]
        both = jnp.maximum(before, top)
        whole = near_sum[h, :, cols] * jnp.exp2((before - both) * SCALE) + total * jnp.exp2((top - both) * SCALE)
        near_t[head_rows(h), cols] = close(whole)

    def far_done(h, cols, top, total):
        rows = pl.ds(pl.multiple_of(h % 2 * HEAD, HEAD), HEAD)
        block = close(total)
        for k in range(QB // (2 * CLUSTER)):
            at = h // 2 * (LANES // 2) + cols.start // (2 * CLUSTER) + k
            far_t[at, rows, :] = block[:, k * 2 * CLUSTER:(k + 1) * 2 * CLUSTER]

    attend(near_q, keys, vals, keep)

    pltpu.make_async_remote_copy(
        src_ref=pool.at[pl.ds(POOLED, ROWS // 2 - POOLED)], dst_ref=pool.at[pl.ds(POOLED, ROWS // 2 - POOLED)],
        send_sem=pout_sems.at[1], recv_sem=pin_sems.at[1], device_id=chip_at(1), device_id_type=MESH,
    ).wait()
    across = pltpu.make_async_remote_copy(
        src_ref=pool.at[pl.ds(0, ROWS // 2)], dst_ref=pool.at[pl.ds(ROWS // 2, ROWS // 2)],
        send_sem=pout_sems.at[0], recv_sem=pin_sems.at[0], device_id=partner, device_id_type=MESH,
    )
    across.start()

    pltpu.make_async_remote_copy(
        src_ref=send.at[pl.ds(2, 2 * LANES - 2)], dst_ref=recv.at[pl.ds(2, 2 * LANES - 2)],
        send_sem=out_sems.at[0], recv_sem=in_sems.at[0], device_id=lane(1), device_id_type=MESH,
    ).wait()
    picks = []
    for j in range(LANES // 2):
        d = jnp.int32(0)
        for k in range(LANES):
            d = d + jnp.where(upto[k] <= j, 1, 0)
        d = jnp.minimum(d, LANES - 1)
        picks.append(d)
        settled[2 * j] = recv[2 * d]
        settled[2 * j + 1] = recv[2 * d + 1]
    project(settled, far_q)
    def back_copy(part, d):
        at = part * LANES + d
        return pltpu.make_async_remote_copy(
            src_ref=back_send.at[at], dst_ref=back_recv.at[at],
            send_sem=bout_sems.at[part], recv_sem=bin_sems.at[part], device_id=lane(-d), device_id_type=MESH,
        )

    def send_back(part):
        for d in range(LANES):
            held = back_recv if d == 0 else back_send
            j = jnp.minimum(upto[d] - active[d], LANES // 2 - 1)
            held[part * LANES + d] = far_t[part * (LANES // 2) + j]
        for d in range(1, LANES):
            back_copy(part, d).start()

    def pooled_here():
        across.wait()
        pool_keys[0] = head_cols(pool, 0)

    def pooled_layout(k):
        if 1 <= k < HEADS:
            pool_keys[k] = head_cols(pool, k)
        elif k in (HEADS, HEADS + 4):
            first_head = k - HEADS
            set_values(pool_vals, pool[:, C + first_head * HEAD:C + (first_head + 4) * HEAD].T, first_head)

    attend(
        far_q, keys, vals, far_done, send_back,
        following=(near_q, pool_keys), before_last=pooled_here, side=pooled_layout,
    )
    send_back(PARTS - 1)

    def returned():
        for part in range(PARTS):
            rest = pl.ds(part * LANES + 1, LANES - 1)
            pltpu.make_async_remote_copy(
                src_ref=back_send.at[rest], dst_ref=back_recv.at[rest],
                send_sem=bout_sems.at[part], recv_sem=bin_sems.at[part], device_id=lane(1), device_id_type=MESH,
            ).wait()

    def turn_back(k):
        if k < LANES // 2:
            block = jnp.concatenate([back_recv[part * LANES + picks[k]] for part in range(PARTS)], axis=0)
            normed[2 * k:2 * k + 2] = block.T.reshape(2, CLUSTER, C)

    attend(near_q, pool_keys, pool_vals, merge, ready=True, before_last=returned, side=turn_back)
    for c in range(CLUSTERS):
        at = jnp.int32(0)
        for j in range(LANES // 2 - 1):
            at = at + jnp.where(picks[j] < offsets[c], 2, 0)
        rank = jnp.int32(0)
        for e in range(c):
            rank = rank + jnp.where(offsets[e] == offsets[c], 1, 0)
        settled[c] = normed[at + jnp.minimum(rank, 1)]
    loads[3].wait()

    def tail(i, _):
        rows = pl.ds(pl.multiple_of(i * ROW_CHUNK, ROW_CHUNK), ROW_CHUNK)
        near = near_t[:, rows].T
        far = settled[pl.ds(i * (ROW_CHUNK // CLUSTER), ROW_CHUNK // CLUSTER)].reshape(ROW_CHUNK, C)
        out[rows, :] = (
            x_ref[rows, :].astype(F32)
            + jnp.dot(near, wout[...], preferred_element_type=F32)
            + jnp.dot(far, wout[...], preferred_element_type=F32)
        ).astype(BF)
        return 0

    lax.fori_loop(0, ROWS // ROW_CHUNK, tail, 0)


def gelu(x):
    half = 0.5 * x
    inner = x * (GELU_A + GELU_B * (x * x))
    return half + half * jnp.tanh(inner)


def mlp_kernel(after_ref, gain_m, wup, wdown, out):
    after = after_ref[...]
    mlp_in = norm_rows(after, gain_m[...])
    total = after.astype(F32)
    for k in range(MLP_SPLIT):
        cols = pl.ds(k * (HIDDEN // MLP_SPLIT), HIDDEN // MLP_SPLIT)
        hidden = gelu(jnp.dot(mlp_in, wup[:, cols], preferred_element_type=F32)).astype(BF)
        total = total + jnp.dot(hidden, wdown[cols, :], preferred_element_type=F32)
    out[...] = total.astype(BF)


def per_device(points, gain_attn, w_query_key, w_value, w_out, gain_mlp, w_up, w_down, cluster_dest):
    vmem = pl.BlockSpec(memory_space=pltpu.VMEM)
    clusters = pltpu.VMEM((CLUSTERS, CLUSTER, C), BF)
    slots = pltpu.VMEM((2 * LANES, CLUSTER, C), BF)
    turned = pltpu.VMEM((C, ROWS), BF)
    parts = pltpu.VMEM((PARTS * LANES, PART, 2 * CLUSTER), BF)
    anywhere = pl.BlockSpec(memory_space=pltpu.HBM)
    moved = (points.reshape(ROWS, C), w_query_key, w_value, w_out, gain_attn.reshape(1, C), cluster_dest.reshape(CLUSTERS))
    moved = tuple(pltpu.with_memory_space_constraint(a, pltpu.HBM) for a in moved)
    after = pl.pallas_call(
        kernel,
        out_shape=jax.ShapeDtypeStruct((ROWS, C), BF),
        in_specs=[anywhere] * 6,
        out_specs=vmem,
        scratch_shapes=[pltpu.VMEM(a.shape, a.dtype) for a in moved[:-1]]
        + [pltpu.SMEM((CLUSTERS,), jnp.int32)]
        + [
            clusters, clusters,
            turned, turned,
            pltpu.VMEM((HEADS, ROWS, HEAD), BF),
            pltpu.VMEM((HEADS, 48, ROWS), BF),
            pltpu.VMEM((HEADS, ROWS, HEAD), BF),
            pltpu.VMEM((HEADS, 48, ROWS), BF),
            pltpu.VMEM((ROWS, 2 * C), BF),
            pltpu.VMEM((2 * GROUP, ROWS, QB), F32),
            pltpu.VMEM((2 * GROUP, ROWS, QB), BF),
            pltpu.VMEM((2 * GROUP, 8, QB), F32),
            pltpu.VMEM((HEADS, 48, ROWS), F32),
            pltpu.VMEM((HEADS, 8, ROWS), F32),
            turned,
            pltpu.VMEM((PARTS * LANES // 2, PART, 2 * CLUSTER), BF),
            slots, slots, parts, parts,
        ]
        + [pltpu.SemaphoreType.DMA((1,))] * 2
        + [pltpu.SemaphoreType.DMA((PARTS,))] * 2
        + [pltpu.SemaphoreType.DMA((2,))] * 2
        + [pltpu.SemaphoreType.DMA((6,))],
        compiler_params=pltpu.CompilerParams(
            collective_id=0, has_side_effects=True, vmem_limit_bytes=40 * 1024 * 1024
        ),
        name="block",
    )(
        *moved
    )
    rows = pl.BlockSpec((MLP_ROWS, C), lambda i: (i, 0))
    result = pl.pallas_call(
        mlp_kernel,
        grid=(ROWS // MLP_ROWS,),
        out_shape=jax.ShapeDtypeStruct((ROWS, C), BF),
        in_specs=[rows] + [vmem] * 3,
        out_specs=rows,
        compiler_params=pltpu.CompilerParams(vmem_limit_bytes=12 * 1024 * 1024),
        name="mlp",
    )(after, gain_mlp.reshape(1, C), w_up, w_down)
    return result.reshape(points.shape)


def solution(mesh):
    placed = (P("ball", "region", None, None),) + (P(),) * 7 + (P("ball", "region", None),)
    return jax.shard_map(
        per_device, mesh=mesh, in_specs=placed, out_specs=P("ball", "region", None, None), check_vma=False
    )
```

```python
import functools
import math

import jax
import jax.numpy as jnp
from jax import lax
from jax.experimental import pallas as pl
from jax.experimental.pallas import tpu as pltpu
from jax.sharding import PartitionSpec as P

MESH = pl.DeviceIdType.MESH
BF = jnp.bfloat16
F32 = jnp.float32
HEADS = 8
HEAD = 32
C = 256
ROWS = 1024
CLUSTER = 64
CLUSTERS = 16
LANES = 16
POOL = 16
POOLED = ROWS // POOL
CHIPS = 8
QB = 512
QBLOCKS = ROWS // QB
BLOCKS = HEADS * QBLOCKS
GROUP = 2
PIECE = 128
DEPTH = 256
PARTS = 4
PART = C // PARTS
HIDDEN = 1024
MLP_ROWS = 512
GELU_A = math.sqrt(2 / math.pi)
GELU_B = GELU_A * 0.044715
MLP_SPLIT = 4
ROW_CHUNK = 256
SCALE = math.log2(math.e) / math.sqrt(HEAD)


def norm_rows(x, gain):
    x = x.astype(F32)
    scale = lax.rsqrt(jnp.mean(x * x, axis=1, keepdims=True) + 1e-6)
    return (x * scale * gain).astype(BF)


def kernel(
    x_in, wqk_in, wv_in, wout_in, gain_in, dest_in, out,
    x_ref, wqk, wv, wout, gain_a, dest,
    normed, settled, near_q, far_q, keys, vals, pool_keys, pool_vals, pool, score, weight, tops, near_sum, near_max, near_t, far_t,
    send, recv, back_send, back_recv,
    out_sems, in_sems, bout_sems, bin_sems, pout_sems, pin_sems, load_sems,
):
    me = lax.axis_index("ball")
    spot = lax.axis_index("region")
    chip, core = spot // 2, spot % 2

    def lane(offset):
        return {"ball": lax.rem(me + offset + LANES, LANES)}

    def chip_at(offset):
        return {"region": lax.rem(chip + offset + CHIPS, CHIPS) * 2 + core}

    partner = {"region": chip * 2 + 1 - core}

    loads = [
        pltpu.make_async_copy(source, held, load_sems.at[k])
        for k, (source, held) in enumerate(
            ((x_in, x_ref), (wqk_in, wqk), (wv_in, wv), (wout_in, wout), (gain_in, gain_a), (dest_in, dest))
        )
    ]
    for k in (5, 4, 0, 1, 2, 3):
        loads[k].start()
    barrier = pltpu.get_barrier_semaphore()
    for d in range(1, LANES):
        pl.semaphore_signal(barrier, inc=1, device_id=lane(d), device_id_type=MESH)
    for d in range(1, CHIPS):
        pl.semaphore_signal(barrier, inc=1, device_id=chip_at(d), device_id_type=MESH)
    pl.semaphore_signal(barrier, inc=1, device_id=partner, device_id_type=MESH)

    loads[5].wait()
    offsets = [lax.bitwise_and(lax.shift_right_arithmetic(dest[c], 4) - me, LANES - 1) for c in range(CLUSTERS)]
    first, second, active, upto = [], [], [], []
    count = jnp.int32(0)
    for d in range(LANES):
        if d == LANES // 2:
            loads[4].wait()
            loads[0].wait()
        lo, hi = jnp.int32(CLUSTERS), jnp.int32(0)
        for c in range(CLUSTERS):
            hi = jnp.where(offsets[c] == d, c, hi)
            lo = jnp.where(offsets[CLUSTERS - 1 - c] == d, CLUSTERS - 1 - c, lo)
        hit = jnp.where(lo < CLUSTERS, 1, 0)
        count = count + hit
        first.append(jnp.minimum(lo, CLUSTERS - 1))
        second.append(hi)
        active.append(hit)
        upto.append(count)


    for c in range(CLUSTERS):
        normed[c] = norm_rows(x_ref[c * CLUSTER:(c + 1) * CLUSTER, :], gain_a[...])
    for d in range(LANES):
        held = recv if d == 0 else send
        held[2 * d] = normed[first[d]]
        held[2 * d + 1] = normed[second[d]]

    pl.semaphore_wait(barrier, LANES - 1 + CHIPS - 1 + 1)
    for d in range(1, LANES):
        copy = pltpu.make_async_remote_copy(
            src_ref=send.at[pl.ds(2 * d, 2)], dst_ref=recv.at[pl.ds(2 * d, 2)],
            send_sem=out_sems.at[0], recv_sem=in_sems.at[0], device_id=lane(d), device_id_type=MESH,
        )
        copy.start()

    def head_cols(rows, h):
        start = h % 4 * HEAD
        half = rows[:, h // 4 * 128:(h // 4 + 1) * 128]
        return (pltpu.roll(half, 128 - start, axis=1) if start else half)[:, :HEAD]

    def set_keys(rows):
        for h in range(HEADS):
            keys[h] = head_cols(rows, h)

    def set_values(held, value_t, first_head=0):
        for h in range(value_t.shape[0] // HEAD):
            held[first_head + h, :HEAD, :] = value_t[h * HEAD:(h + 1) * HEAD, :]

    def project(source, query_t):
        states = source[...].reshape(ROWS, C)
        turned = states.T
        query_t[...] = jnp.dot(wqk[:, :C].T, turned, preferred_element_type=F32).astype(BF)
        key_rows = jnp.dot(states, wqk[:, C:], preferred_element_type=F32).astype(BF)
        set_keys(key_rows)
        set_values(vals, jnp.dot(wv[...].T, turned, preferred_element_type=F32).astype(BF))
        return key_rows

    for h in range(HEADS):
        vals[h, HEAD:, :] = jnp.ones((16, ROWS), BF)
        pool_vals[h, HEAD:, :] = jnp.ones((16, ROWS), BF)
    for load in loads[1:3]:
        load.wait()
    key_rows = project(normed, near_q)

    row = lax.broadcasted_iota(jnp.int32, (POOLED, ROWS), 0)
    col = lax.broadcasted_iota(jnp.int32, (POOLED, ROWS), 1)
    pooling = jnp.where(col // POOL == row, 1.0 / math.sqrt(POOL), 0.0).astype(BF)
    pool[:POOLED, :C] = jnp.dot(pooling, key_rows, preferred_element_type=F32).astype(BF)
    value_rows = jnp.dot(normed[...].reshape(ROWS, C), wv[...], preferred_element_type=F32).astype(BF)
    pool[:POOLED, C:] = jnp.dot(pooling, value_rows, preferred_element_type=F32).astype(BF)
    for d in range(1, CHIPS):
        copy = pltpu.make_async_remote_copy(
            src_ref=pool.at[pl.ds(0, POOLED)], dst_ref=pool.at[pl.ds(d * POOLED, POOLED)],
            send_sem=pout_sems.at[1], recv_sem=pin_sems.at[1], device_id=chip_at(d), device_id_type=MESH,
        )
        copy.start()

    def attend(query_t, keys, vals, finish, between=None, ready=False, following=None, before_last=None, side=None):
        def spot_of(i):
            return i // QBLOCKS, pl.ds(pl.multiple_of(i % QBLOCKS * QB, QB), QB)

        def head_rows(h):
            return pl.ds(pl.multiple_of(h * HEAD, HEAD), HEAD)

        def scores_of(i, slot, r, top, query_t=query_t, keys=keys):
            h, cols = spot_of(i)
            rows = pl.ds(r * PIECE, PIECE)
            s = jnp.dot(keys[h, rows, :], query_t[head_rows(h), cols], preferred_element_type=F32)
            score[slot, rows, :] = s
            for j in range(PIECE // 8):
                top = jnp.maximum(top, s[j * 8:(j + 1) * 8])
            return top

        def sum_of(h, slot, c, total):
            rows = pl.ds(c * DEPTH, DEPTH)
            return total + jnp.dot(vals[h, :, rows], weight[slot, rows, :], preferred_element_type=F32)

        def top_of(slot):
            return jnp.max(tops[slot], axis=0, keepdims=True)

        low = jnp.full((8, QB), -jnp.inf, F32)
        none = jnp.zeros((48, QB), F32)

        def step(g, even, last=False):
            for b in range(GROUP):
                i = g * GROUP + b
                now = b if even else GROUP + b
                other = GROUP + b if even else b
                old = jnp.maximum(i - GROUP, 0)
                new = jnp.minimum(i + GROUP, BLOCKS - 1)
                old_head, old_cols = spot_of(old)
                head, cols = spot_of(i)
                old_top = top_of(other)
                top = top_of(now)
                new_top, total, last_total = low, none, none
                for r in range(ROWS // PIECE):
                    rows = pl.ds(r * PIECE, PIECE)
                    if not last:
                        new_top = scores_of(new, other, r, new_top)
                    else:
                        if side is not None:
                            side(b * (ROWS // PIECE) + r)
                        if following is not None:
                            new_top = scores_of(b, other, r, new_top, *following)
                    weight[now, rows, :] = jnp.exp2((score[now, rows, :] - top) * SCALE).astype(BF)
                    if (r + 1) * PIECE % DEPTH == 0:
                        part = (r + 1) * PIECE // DEPTH - 1
                        total = sum_of(old_head, other, part, total)
                        if last:
                            last_total = sum_of(head, now, part, last_total)
                finish(old_head, old_cols, old_top, total)
                if last:
                    finish(head, cols, top, last_total)
                if not last or following is not None:
                    tops[other] = new_top

        for b in range(0 if ready else GROUP):
            top = low
            for r in range(ROWS // PIECE):
                top = scores_of(b, b, r, top)
            tops[b] = top

        pairs = BLOCKS // GROUP // 2

        def pair(t, _):
            @pl.when(t < pairs)
            def _():
                step(2 * t, True)

            if between is not None:
                @pl.when(t >= 1)
                def _():
                    between(t - 1)

            @pl.when(t < pairs - 1)
            def _():
                step(2 * t + 1, False)

            if before_last is not None:
                pl.when(t == pairs - 1)(before_last)

            @pl.when(t == pairs - 1)
            def _():
                step(2 * t + 1, False, last=True)

            return 0

        lax.fori_loop(0, pairs, pair, 0)

    def keep(h, cols, top, total):
        near_sum[h, :, cols] = total
        near_max[h, :, cols] = jnp.broadcast_to(top, (8, QB))

    def head_rows(h):
        return pl.ds(pl.multiple_of(h * HEAD, HEAD), HEAD)

    def close(total):
        return (total[:HEAD] / total[HEAD:HEAD + 1]).astype(BF)

    def merge(h, cols, top, total):
        before = near_max[h, :1, cols]
        both = jnp.maximum(before, top)
        whole = near_sum[h, :, cols] * jnp.exp2((before - both) * SCALE) + total * jnp.exp2((top - both) * SCALE)
        near_t[head_rows(h), cols] = close(whole)

    def far_done(h, cols, top, total):
        rows = pl.ds(pl.multiple_of(h % 2 * HEAD, HEAD), HEAD)
        block = close(total)
        for k in range(QB // (2 * CLUSTER)):
            at = h // 2 * (LANES // 2) + cols.start // (2 * CLUSTER) + k
            far_t[at, rows, :] = block[:, k * 2 * CLUSTER:(k + 1) * 2 * CLUSTER]

    attend(near_q, keys, vals, keep)

    pltpu.make_async_remote_copy(
        src_ref=pool.at[pl.ds(POOLED, ROWS // 2 - POOLED)], dst_ref=pool.at[pl.ds(POOLED, ROWS // 2 - POOLED)],
        send_sem=pout_sems.at[1], recv_sem=pin_sems.at[1], device_id=chip_at(1), device_id_type=MESH,
    ).wait()
    across = pltpu.make_async_remote_copy(
        src_ref=pool.at[pl.ds(0, ROWS // 2)], dst_ref=pool.at[pl.ds(ROWS // 2, ROWS // 2)],
        send_sem=pout_sems.at[0], recv_sem=pin_sems.at[0], device_id=partner, device_id_type=MESH,
    )
    across.start()

    picks = []
    for j in range(LANES // 2):
        d = jnp.int32(0)
        for k in range(LANES):
            d = d + jnp.where(upto[k] <= j, 1, 0)
        picks.append(jnp.minimum(d, LANES - 1))

    pltpu.make_async_remote_copy(
        src_ref=send.at[pl.ds(2, 2 * LANES - 2)], dst_ref=recv.at[pl.ds(2, 2 * LANES - 2)],
        send_sem=out_sems.at[0], recv_sem=in_sems.at[0], device_id=lane(1), device_id_type=MESH,
    ).wait()
    for j in range(LANES // 2):
        settled[2 * j] = recv[2 * picks[j]]
        settled[2 * j + 1] = recv[2 * picks[j] + 1]
    project(settled, far_q)
    def back_copy(part, d):
        at = part * LANES + d
        return pltpu.make_async_remote_copy(
            src_ref=back_send.at[at], dst_ref=back_recv.at[at],
            send_sem=bout_sems.at[part], recv_sem=bin_sems.at[part], device_id=lane(-d), device_id_type=MESH,
        )

    def send_back(part):
        for d in range(LANES):
            held = back_recv if d == 0 else back_send
            j = jnp.minimum(upto[d] - active[d], LANES // 2 - 1)
            held[part * LANES + d] = far_t[part * (LANES // 2) + j]
        for d in range(1, LANES):
            back_copy(part, d).start()

    def pooled_here():
        across.wait()
        pool_keys[0] = head_cols(pool, 0)

    def pooled_layout(k):
        if 1 <= k < HEADS:
            pool_keys[k] = head_cols(pool, k)
        elif k in (HEADS, HEADS + 4):
            first_head = k - HEADS
            set_values(pool_vals, pool[:, C + first_head * HEAD:C + (first_head + 4) * HEAD].T, first_head)

    attend(
        far_q, keys, vals, far_done, send_back,
        following=(near_q, pool_keys), before_last=pooled_here, side=pooled_layout,
    )
    send_back(PARTS - 1)

    def returned():
        for part in range(PARTS):
            rest = pl.ds(part * LANES + 1, LANES - 1)
            pltpu.make_async_remote_copy(
                src_ref=back_send.at[rest], dst_ref=back_recv.at[rest],
                send_sem=bout_sems.at[part], recv_sem=bin_sems.at[part], device_id=lane(1), device_id_type=MESH,
            ).wait()

    def turn_back(k):
        if k < LANES // 2:
            block = jnp.concatenate([back_recv[part * LANES + picks[k]] for part in range(PARTS)], axis=0)
            normed[2 * k:2 * k + 2] = block.T.reshape(2, CLUSTER, C)

    attend(near_q, pool_keys, pool_vals, merge, ready=True, before_last=returned, side=turn_back)
    loads[3].wait()
    for i in range(ROWS // ROW_CHUNK):
        rows = slice(i * ROW_CHUNK, (i + 1) * ROW_CHUNK)
        per_chunk = ROW_CHUNK // CLUSTER
        for c in range(i * per_chunk, (i + 1) * per_chunk):
            at = jnp.int32(0)
            for j in range(LANES // 2 - 1):
                at = at + jnp.where(picks[j] < offsets[c], 2, 0)
            rank = jnp.int32(0)
            for e in range(c):
                rank = rank + jnp.where(offsets[e] == offsets[c], 1, 0)
            settled[c] = normed[at + jnp.minimum(rank, 1)]
        far = settled[i * per_chunk:(i + 1) * per_chunk].reshape(ROW_CHUNK, C)
        out[rows, :] = (
            x_ref[rows, :].astype(F32)
            + jnp.dot(near_t[:, rows].T, wout[...], preferred_element_type=F32)
            + jnp.dot(far, wout[...], preferred_element_type=F32)
        ).astype(BF)


def gelu(x):
    half = 0.5 * x
    inner = x * (GELU_A + GELU_B * (x * x))
    return half + half * jnp.tanh(inner)


def mlp_kernel(after_ref, gain_m, wup, wdown, out):
    after = after_ref[...]
    mlp_in = norm_rows(after, gain_m[...])
    total = after.astype(F32)
    for k in range(MLP_SPLIT):
        cols = pl.ds(k * (HIDDEN // MLP_SPLIT), HIDDEN // MLP_SPLIT)
        hidden = gelu(jnp.dot(mlp_in, wup[:, cols], preferred_element_type=F32)).astype(BF)
        total = total + jnp.dot(hidden, wdown[cols, :], preferred_element_type=F32)
    out[...] = total.astype(BF)


def per_device(points, gain_attn, w_query_key, w_value, w_out, gain_mlp, w_up, w_down, cluster_dest):
    vmem = pl.BlockSpec(memory_space=pltpu.VMEM)
    clusters = pltpu.VMEM((CLUSTERS, CLUSTER, C), BF)
    slots = pltpu.VMEM((2 * LANES, CLUSTER, C), BF)
    turned = pltpu.VMEM((C, ROWS), BF)
    parts = pltpu.VMEM((PARTS * LANES, PART, 2 * CLUSTER), BF)
    anywhere = pl.BlockSpec(memory_space=pltpu.HBM)
    moved = (points.reshape(ROWS, C), w_query_key, w_value, w_out, gain_attn.reshape(1, C), cluster_dest.reshape(CLUSTERS))
    moved = tuple(pltpu.with_memory_space_constraint(a, pltpu.HBM) for a in moved)
    after = pl.pallas_call(
        kernel,
        out_shape=jax.ShapeDtypeStruct((ROWS, C), BF),
        in_specs=[anywhere] * 6,
        out_specs=vmem,
        scratch_shapes=[pltpu.VMEM(a.shape, a.dtype) for a in moved[:-1]]
        + [pltpu.SMEM((CLUSTERS,), jnp.int32)]
        + [
            clusters, clusters,
            turned, turned,
            pltpu.VMEM((HEADS, ROWS, HEAD), BF),
            pltpu.VMEM((HEADS, 48, ROWS), BF),
            pltpu.VMEM((HEADS, ROWS, HEAD), BF),
            pltpu.VMEM((HEADS, 48, ROWS), BF),
            pltpu.VMEM((ROWS, 2 * C), BF),
            pltpu.VMEM((2 * GROUP, ROWS, QB), F32),
            pltpu.VMEM((2 * GROUP, ROWS, QB), BF),
            pltpu.VMEM((2 * GROUP, 8, QB), F32),
            pltpu.VMEM((HEADS, 48, ROWS), F32),
            pltpu.VMEM((HEADS, 8, ROWS), F32),
            turned,
            pltpu.VMEM((PARTS * LANES // 2, PART, 2 * CLUSTER), BF),
            slots, slots, parts, parts,
        ]
        + [pltpu.SemaphoreType.DMA((1,))] * 2
        + [pltpu.SemaphoreType.DMA((PARTS,))] * 2
        + [pltpu.SemaphoreType.DMA((2,))] * 2
        + [pltpu.SemaphoreType.DMA((6,))],
        compiler_params=pltpu.CompilerParams(
            collective_id=0, has_side_effects=True, vmem_limit_bytes=40 * 1024 * 1024
        ),
        name="block",
    )(
        *moved
    )
    rows = pl.BlockSpec((MLP_ROWS, C), lambda i: (i, 0))
    result = pl.pallas_call(
        mlp_kernel,
        grid=(ROWS // MLP_ROWS,),
        out_shape=jax.ShapeDtypeStruct((ROWS, C), BF),
        in_specs=[rows] + [vmem] * 3,
        out_specs=rows,
        compiler_params=pltpu.CompilerParams(vmem_limit_bytes=12 * 1024 * 1024),
        name="mlp",
    )(after, gain_mlp.reshape(1, C), w_up, w_down)
    return result.reshape(points.shape)


def solution(mesh):
    placed = (P("ball", "region", None, None),) + (P(),) * 7 + (P("ball", "region", None),)
    return jax.shard_map(
        per_device, mesh=mesh, in_specs=placed, out_specs=P("ball", "region", None, None), check_vma=False
    )
```

```python
import functools
import math

import jax
import jax.numpy as jnp
from jax import lax
from jax.experimental import pallas as pl
from jax.experimental.pallas import tpu as pltpu
from jax.sharding import PartitionSpec as P

MESH = pl.DeviceIdType.MESH
BF = jnp.bfloat16
F32 = jnp.float32
HEADS = 8
HEAD = 32
C = 256
ROWS = 1024
CLUSTER = 64
CLUSTERS = 16
LANES = 16
POOL = 16
POOLED = ROWS // POOL
CHIPS = 8
FAR_FIRST = (10, 9, 11, 6, 14, 5, 7, 13, 15, 2, 8, 1, 3, 4, 12)
CHIPS_FAR_FIRST = (4, 3, 5, 2, 6, 1, 7)
QB = 512
QBLOCKS = ROWS // QB
BLOCKS = HEADS * QBLOCKS
GROUP = 2
PIECE = 128
DEPTH = 256
PARTS = 4
PART = C // PARTS
HIDDEN = 1024
MLP_ROWS = 512
GELU_A = math.sqrt(2 / math.pi)
GELU_B = GELU_A * 0.044715
MLP_SPLIT = 4
ROW_CHUNK = 256
SCALE = math.log2(math.e) / math.sqrt(HEAD)


def norm_rows(x, gain):
    x = x.astype(F32)
    scale = lax.rsqrt(jnp.mean(x * x, axis=1, keepdims=True) + 1e-6)
    return (x * scale * gain).astype(BF)


def kernel(
    x_in, wqk_in, wv_in, wout_in, gain_in, dest_in, out,
    x_ref, wqk, wv, wout, gain_a, dest,
    normed, settled, near_q, far_q, keys, vals, pool_keys, pool_vals, pool, score, weight, tops, near_sum, near_max, near_t, far_t,
    send, recv, back_send, back_recv,
    out_sems, in_sems, bout_sems, bin_sems, pout_sems, pin_sems, load_sems,
):
    me = lax.axis_index("ball")
    spot = lax.axis_index("region")
    chip, core = spot // 2, spot % 2

    def lane(offset):
        return {"ball": lax.rem(me + offset + LANES, LANES)}

    def chip_at(offset):
        return {"region": lax.rem(chip + offset + CHIPS, CHIPS) * 2 + core}

    partner = {"region": chip * 2 + 1 - core}

    loads = [
        pltpu.make_async_copy(source, held, load_sems.at[k])
        for k, (source, held) in enumerate(
            ((x_in, x_ref), (wqk_in, wqk), (wv_in, wv), (wout_in, wout), (gain_in, gain_a), (dest_in, dest))
        )
    ]
    for k in (5, 4, 0, 1, 2, 3):
        loads[k].start()
    barrier = pltpu.get_barrier_semaphore()
    pl.semaphore_signal(barrier, inc=1, device_id=lane(FAR_FIRST[0]), device_id_type=MESH)
    for d in CHIPS_FAR_FIRST[:3]:
        pl.semaphore_signal(barrier, inc=1, device_id=chip_at(d), device_id_type=MESH)
    for d in FAR_FIRST[1:]:
        pl.semaphore_signal(barrier, inc=1, device_id=lane(d), device_id_type=MESH)
    for d in CHIPS_FAR_FIRST[3:]:
        pl.semaphore_signal(barrier, inc=1, device_id=chip_at(d), device_id_type=MESH)
    pl.semaphore_signal(barrier, inc=1, device_id=partner, device_id_type=MESH)

    loads[5].wait()
    offsets = [lax.bitwise_and(lax.shift_right_arithmetic(dest[c], 4) - me, LANES - 1) for c in range(CLUSTERS)]
    first, second, active, upto = [], [], [], []
    count = jnp.int32(0)
    for d in range(LANES):
        if d == LANES // 2:
            loads[4].wait()
            loads[0].wait()
        lo, hi = jnp.int32(CLUSTERS), jnp.int32(0)
        for c in range(CLUSTERS):
            hi = jnp.where(offsets[c] == d, c, hi)
            lo = jnp.where(offsets[CLUSTERS - 1 - c] == d, CLUSTERS - 1 - c, lo)
        hit = jnp.where(lo < CLUSTERS, 1, 0)
        count = count + hit
        first.append(jnp.minimum(lo, CLUSTERS - 1))
        second.append(hi)
        active.append(hit)
        upto.append(count)


    for c in range(CLUSTERS):
        normed[c] = norm_rows(x_ref[c * CLUSTER:(c + 1) * CLUSTER, :], gain_a[...])
    for d in range(LANES):
        held = recv if d == 0 else send
        held[2 * d] = normed[first[d]]
        held[2 * d + 1] = normed[second[d]]

    pl.semaphore_wait(barrier, LANES - 1 + CHIPS - 1 + 1)
    for d in FAR_FIRST:
        copy = pltpu.make_async_remote_copy(
            src_ref=send.at[pl.ds(2 * d, 2)], dst_ref=recv.at[pl.ds(2 * d, 2)],
            send_sem=out_sems.at[0], recv_sem=in_sems.at[0], device_id=lane(d), device_id_type=MESH,
        )
        copy.start()

    def head_cols(rows, h):
        start = h % 4 * HEAD
        half = rows[:, h // 4 * 128:(h // 4 + 1) * 128]
        return (pltpu.roll(half, 128 - start, axis=1) if start else half)[:, :HEAD]

    def set_keys(rows):
        for h in range(HEADS):
            keys[h] = head_cols(rows, h)

    def set_values(held, value_t, first_head=0):
        for h in range(value_t.shape[0] // HEAD):
            held[first_head + h, :HEAD, :] = value_t[h * HEAD:(h + 1) * HEAD, :]

    def project(source, query_t):
        states = source[...].reshape(ROWS, C)
        turned = states.T
        query_t[...] = jnp.dot(wqk[:, :C].T, turned, preferred_element_type=F32).astype(BF)
        key_rows = jnp.dot(states, wqk[:, C:], preferred_element_type=F32).astype(BF)
        set_keys(key_rows)
        set_values(vals, jnp.dot(wv[...].T, turned, preferred_element_type=F32).astype(BF))
        return key_rows

    for h in range(HEADS):
        vals[h, HEAD:, :] = jnp.ones((16, ROWS), BF)
        pool_vals[h, HEAD:, :] = jnp.ones((16, ROWS), BF)
    for load in loads[1:3]:
        load.wait()
    key_rows = project(normed, near_q)

    row = lax.broadcasted_iota(jnp.int32, (POOLED, ROWS), 0)
    col = lax.broadcasted_iota(jnp.int32, (POOLED, ROWS), 1)
    pooling = jnp.where(col // POOL == row, 1.0 / math.sqrt(POOL), 0.0).astype(BF)
    pool[:POOLED, :C] = jnp.dot(pooling, key_rows, preferred_element_type=F32).astype(BF)
    value_rows = jnp.dot(normed[...].reshape(ROWS, C), wv[...], preferred_element_type=F32).astype(BF)
    pool[:POOLED, C:] = jnp.dot(pooling, value_rows, preferred_element_type=F32).astype(BF)
    for d in CHIPS_FAR_FIRST:
        copy = pltpu.make_async_remote_copy(
            src_ref=pool.at[pl.ds(0, POOLED)], dst_ref=pool.at[pl.ds(d * POOLED, POOLED)],
            send_sem=pout_sems.at[1], recv_sem=pin_sems.at[1], device_id=chip_at(d), device_id_type=MESH,
        )
        copy.start()

    def attend(query_t, keys, vals, finish, between=None, ready=False, following=None, before_last=None, side=None):
        def spot_of(i):
            return i // QBLOCKS, pl.ds(pl.multiple_of(i % QBLOCKS * QB, QB), QB)

        def head_rows(h):
            return pl.ds(pl.multiple_of(h * HEAD, HEAD), HEAD)

        def scores_of(i, slot, r, top, query_t=query_t, keys=keys):
            h, cols = spot_of(i)
            rows = pl.ds(r * PIECE, PIECE)
            s = jnp.dot(keys[h, rows, :], query_t[head_rows(h), cols], preferred_element_type=F32)
            score[slot, rows, :] = s
            for j in range(PIECE // 8):
                top = jnp.maximum(top, s[j * 8:(j + 1) * 8])
            return top

        def sum_of(h, slot, c, total):
            rows = pl.ds(c * DEPTH, DEPTH)
            return total + jnp.dot(vals[h, :, rows], weight[slot, rows, :], preferred_element_type=F32)

        def top_of(slot):
            return jnp.max(tops[slot], axis=0, keepdims=True)

        low = jnp.full((8, QB), -jnp.inf, F32)
        none = jnp.zeros((48, QB), F32)

        def step(g, even, last=False):
            for b in range(GROUP):
                i = g * GROUP + b
                now = b if even else GROUP + b
                other = GROUP + b if even else b
                old = jnp.maximum(i - GROUP, 0)
                new = jnp.minimum(i + GROUP, BLOCKS - 1)
                old_head, old_cols = spot_of(old)
                head, cols = spot_of(i)
                old_top = top_of(other)
                top = top_of(now)
                new_top, total, last_total = low, none, none
                for r in range(ROWS // PIECE):
                    rows = pl.ds(r * PIECE, PIECE)
                    if not last:
                        new_top = scores_of(new, other, r, new_top)
                    else:
                        if side is not None:
                            side(b * (ROWS // PIECE) + r)
                        if following is not None:
                            new_top = scores_of(b, other, r, new_top, *following)
                    weight[now, rows, :] = jnp.exp2((score[now, rows, :] - top) * SCALE).astype(BF)
                    if (r + 1) * PIECE % DEPTH == 0:
                        part = (r + 1) * PIECE // DEPTH - 1
                        total = sum_of(old_head, other, part, total)
                        if last:
                            last_total = sum_of(head, now, part, last_total)
                finish(old_head, old_cols, old_top, total)
                if last:
                    finish(head, cols, top, last_total)
                if not last or following is not None:
                    tops[other] = new_top

        for b in range(0 if ready else GROUP):
            top = low
            for r in range(ROWS // PIECE):
                top = scores_of(b, b, r, top)
            tops[b] = top

        pairs = BLOCKS // GROUP // 2

        def pair(t, _):
            @pl.when(t < pairs)
            def _():
                step(2 * t, True)

            if between is not None:
                @pl.when(t >= 1)
                def _():
                    between(t - 1)

            @pl.when(t < pairs - 1)
            def _():
                step(2 * t + 1, False)

            if before_last is not None:
                pl.when(t == pairs - 1)(before_last)

            @pl.when(t == pairs - 1)
            def _():
                step(2 * t + 1, False, last=True)

            return 0

        lax.fori_loop(0, pairs, pair, 0)

    def keep(h, cols, top, total):
        near_sum[h, :, cols] = total
        near_max[h, :, cols] = jnp.broadcast_to(top, (8, QB))

    def head_rows(h):
        return pl.ds(pl.multiple_of(h * HEAD, HEAD), HEAD)

    def close(total):
        return (total[:HEAD] / total[HEAD:HEAD + 1]).astype(BF)

    def merge(h, cols, top, total):
        before = near_max[h, :1, cols]
        both = jnp.maximum(before, top)
        whole = near_sum[h, :, cols] * jnp.exp2((before - both) * SCALE) + total * jnp.exp2((top - both) * SCALE)
        near_t[head_rows(h), cols] = close(whole)

    def far_done(h, cols, top, total):
        rows = pl.ds(pl.multiple_of(h % 2 * HEAD, HEAD), HEAD)
        block = close(total)
        for k in range(QB // (2 * CLUSTER)):
            at = h // 2 * (LANES // 2) + cols.start // (2 * CLUSTER) + k
            far_t[at, rows, :] = block[:, k * 2 * CLUSTER:(k + 1) * 2 * CLUSTER]

    attend(near_q, keys, vals, keep)

    pltpu.make_async_remote_copy(
        src_ref=pool.at[pl.ds(POOLED, ROWS // 2 - POOLED)], dst_ref=pool.at[pl.ds(POOLED, ROWS // 2 - POOLED)],
        send_sem=pout_sems.at[1], recv_sem=pin_sems.at[1], device_id=chip_at(1), device_id_type=MESH,
    ).wait()
    across = pltpu.make_async_remote_copy(
        src_ref=pool.at[pl.ds(0, ROWS // 2)], dst_ref=pool.at[pl.ds(ROWS // 2, ROWS // 2)],
        send_sem=pout_sems.at[0], recv_sem=pin_sems.at[0], device_id=partner, device_id_type=MESH,
    )
    across.start()

    picks = []
    for j in range(LANES // 2):
        d = jnp.int32(0)
        for k in range(LANES):
            d = d + jnp.where(upto[k] <= j, 1, 0)
        picks.append(jnp.minimum(d, LANES - 1))

    pltpu.make_async_remote_copy(
        src_ref=send.at[pl.ds(2, 2 * LANES - 2)], dst_ref=recv.at[pl.ds(2, 2 * LANES - 2)],
        send_sem=out_sems.at[0], recv_sem=in_sems.at[0], device_id=lane(1), device_id_type=MESH,
    ).wait()
    for j in range(LANES // 2):
        settled[2 * j] = recv[2 * picks[j]]
        settled[2 * j + 1] = recv[2 * picks[j] + 1]
    project(settled, far_q)
    def back_copy(part, d):
        at = part * LANES + d
        return pltpu.make_async_remote_copy(
            src_ref=back_send.at[at], dst_ref=back_recv.at[at],
            send_sem=bout_sems.at[part], recv_sem=bin_sems.at[part], device_id=lane(-d), device_id_type=MESH,
        )

    def send_back(part):
        for d in range(LANES):
            held = back_recv if d == 0 else back_send
            j = jnp.minimum(upto[d] - active[d], LANES // 2 - 1)
            held[part * LANES + d] = far_t[part * (LANES // 2) + j]
        for d in FAR_FIRST:
            back_copy(part, d).start()

    def pooled_here():
        across.wait()
        pool_keys[0] = head_cols(pool, 0)

    def pooled_layout(k):
        if 1 <= k < HEADS:
            pool_keys[k] = head_cols(pool, k)
        elif k in (HEADS, HEADS + 4):
            first_head = k - HEADS
            set_values(pool_vals, pool[:, C + first_head * HEAD:C + (first_head + 4) * HEAD].T, first_head)

    attend(
        far_q, keys, vals, far_done, send_back,
        following=(near_q, pool_keys), before_last=pooled_here, side=pooled_layout,
    )
    send_back(PARTS - 1)

    def returned():
        for part in range(PARTS):
            rest = pl.ds(part * LANES + 1, LANES - 1)
            pltpu.make_async_remote_copy(
                src_ref=back_send.at[rest], dst_ref=back_recv.at[rest],
                send_sem=bout_sems.at[part], recv_sem=bin_sems.at[part], device_id=lane(1), device_id_type=MESH,
            ).wait()

    def turn_back(k):
        if k < LANES // 2:
            block = jnp.concatenate([back_recv[part * LANES + picks[k]] for part in range(PARTS)], axis=0)
            normed[2 * k:2 * k + 2] = block.T.reshape(2, CLUSTER, C)

    attend(near_q, pool_keys, pool_vals, merge, ready=True, before_last=returned, side=turn_back)
    loads[3].wait()
    for i in range(ROWS // ROW_CHUNK):
        rows = slice(i * ROW_CHUNK, (i + 1) * ROW_CHUNK)
        per_chunk = ROW_CHUNK // CLUSTER
        for c in range(i * per_chunk, (i + 1) * per_chunk):
            at = jnp.int32(0)
            for j in range(LANES // 2 - 1):
                at = at + jnp.where(picks[j] < offsets[c], 2, 0)
            rank = jnp.int32(0)
            for e in range(c):
                rank = rank + jnp.where(offsets[e] == offsets[c], 1, 0)
            settled[c] = normed[at + jnp.minimum(rank, 1)]
        far = settled[i * per_chunk:(i + 1) * per_chunk].reshape(ROW_CHUNK, C)
        out[rows, :] = (
            x_ref[rows, :].astype(F32)
            + jnp.dot(near_t[:, rows].T, wout[...], preferred_element_type=F32)
            + jnp.dot(far, wout[...], preferred_element_type=F32)
        ).astype(BF)


def gelu(x):
    half = 0.5 * x
    inner = x * (GELU_A + GELU_B * (x * x))
    return half + half * jnp.tanh(inner)


def mlp_kernel(after_ref, gain_m, wup, wdown, out):
    after = after_ref[...]
    mlp_in = norm_rows(after, gain_m[...])
    total = after.astype(F32)
    for k in range(MLP_SPLIT):
        cols = pl.ds(k * (HIDDEN // MLP_SPLIT), HIDDEN // MLP_SPLIT)
        hidden = gelu(jnp.dot(mlp_in, wup[:, cols], preferred_element_type=F32)).astype(BF)
        total = total + jnp.dot(hidden, wdown[cols, :], preferred_element_type=F32)
    out[...] = total.astype(BF)


def per_device(points, gain_attn, w_query_key, w_value, w_out, gain_mlp, w_up, w_down, cluster_dest):
    vmem = pl.BlockSpec(memory_space=pltpu.VMEM)
    clusters = pltpu.VMEM((CLUSTERS, CLUSTER, C), BF)
    slots = pltpu.VMEM((2 * LANES, CLUSTER, C), BF)
    turned = pltpu.VMEM((C, ROWS), BF)
    parts = pltpu.VMEM((PARTS * LANES, PART, 2 * CLUSTER), BF)
    anywhere = pl.BlockSpec(memory_space=pltpu.HBM)
    moved = (points.reshape(ROWS, C), w_query_key, w_value, w_out, gain_attn.reshape(1, C), cluster_dest.reshape(CLUSTERS))
    moved = tuple(pltpu.with_memory_space_constraint(a, pltpu.HBM) for a in moved)
    after = pl.pallas_call(
        kernel,
        out_shape=jax.ShapeDtypeStruct((ROWS, C), BF),
        in_specs=[anywhere] * 6,
        out_specs=vmem,
        scratch_shapes=[pltpu.VMEM(a.shape, a.dtype) for a in moved[:-1]]
        + [pltpu.SMEM((CLUSTERS,), jnp.int32)]
        + [
            clusters, clusters,
            turned, turned,
            pltpu.VMEM((HEADS, ROWS, HEAD), BF),
            pltpu.VMEM((HEADS, 48, ROWS), BF),
            pltpu.VMEM((HEADS, ROWS, HEAD), BF),
            pltpu.VMEM((HEADS, 48, ROWS), BF),
            pltpu.VMEM((ROWS, 2 * C), BF),
            pltpu.VMEM((2 * GROUP, ROWS, QB), F32),
            pltpu.VMEM((2 * GROUP, ROWS, QB), BF),
            pltpu.VMEM((2 * GROUP, 8, QB), F32),
            pltpu.VMEM((HEADS, 48, ROWS), F32),
            pltpu.VMEM((HEADS, 8, ROWS), F32),
            turned,
            pltpu.VMEM((PARTS * LANES // 2, PART, 2 * CLUSTER), BF),
            slots, slots, parts, parts,
        ]
        + [pltpu.SemaphoreType.DMA((1,))] * 2
        + [pltpu.SemaphoreType.DMA((PARTS,))] * 2
        + [pltpu.SemaphoreType.DMA((2,))] * 2
        + [pltpu.SemaphoreType.DMA((6,))],
        compiler_params=pltpu.CompilerParams(
            collective_id=0, has_side_effects=True, vmem_limit_bytes=40 * 1024 * 1024
        ),
        name="block",
    )(
        *moved
    )
    rows = pl.BlockSpec((MLP_ROWS, C), lambda i: (i, 0))
    result = pl.pallas_call(
        mlp_kernel,
        grid=(ROWS // MLP_ROWS,),
        out_shape=jax.ShapeDtypeStruct((ROWS, C), BF),
        in_specs=[rows] + [vmem] * 3,
        out_specs=rows,
        compiler_params=pltpu.CompilerParams(vmem_limit_bytes=12 * 1024 * 1024),
        name="mlp",
    )(after, gain_mlp.reshape(1, C), w_up, w_down)
    return result.reshape(points.shape)


def solution(mesh):
    placed = (P("ball", "region", None, None),) + (P(),) * 7 + (P("ball", "region", None),)
    return jax.shard_map(
        per_device, mesh=mesh, in_specs=placed, out_specs=P("ball", "region", None, None), check_vma=False
    )
```

```python
import functools
import math

import jax
import jax.numpy as jnp
from jax import lax
from jax.experimental import pallas as pl
from jax.experimental.pallas import tpu as pltpu
from jax.sharding import PartitionSpec as P

MESH = pl.DeviceIdType.MESH
BF = jnp.bfloat16
F32 = jnp.float32
HEADS = 8
HEAD = 32
C = 256
ROWS = 1024
CLUSTER = 64
CLUSTERS = 16
LANES = 16
POOL = 16
POOLED = ROWS // POOL
CHIPS = 8
FAR_FIRST = (10, 9, 11, 6, 14, 5, 7, 13, 15, 2, 8, 1, 3, 4, 12)
CHIPS_FAR_FIRST = (4, 3, 5, 2, 6, 1, 7)
QB = 512
QBLOCKS = ROWS // QB
BLOCKS = HEADS * QBLOCKS
GROUP = 2
PIECE = 128
DEPTH = 256
PARTS = 4
PART = C // PARTS
HIDDEN = 1024
MLP_ROWS = 1024
GELU_A = math.sqrt(2 / math.pi)
GELU_B = GELU_A * 0.044715
MLP_SPLIT = 4
ROW_CHUNK = 256
SCALE = math.log2(math.e) / math.sqrt(HEAD)


def norm_rows(x, gain):
    x = x.astype(F32)
    scale = lax.rsqrt(jnp.mean(x * x, axis=1, keepdims=True) + 1e-6)
    return (x * scale * gain).astype(BF)


def kernel(
    x_in, wqk_in, wv_in, wout_in, gain_in, dest_in, out,
    x_ref, wqk, wv, wout, gain_a, dest,
    normed, settled, near_q, far_q, keys, vals, pool_keys, pool_vals, pool, score, weight, tops, near_sum, near_max, near_t, far_t,
    send, recv, back_send, back_recv,
    out_sems, in_sems, bout_sems, bin_sems, pout_sems, pin_sems, load_sems,
):
    me = lax.axis_index("ball")
    spot = lax.axis_index("region")
    chip, core = spot // 2, spot % 2

    def lane(offset):
        return {"ball": lax.rem(me + offset + LANES, LANES)}

    def chip_at(offset):
        return {"region": lax.rem(chip + offset + CHIPS, CHIPS) * 2 + core}

    partner = {"region": chip * 2 + 1 - core}

    loads = [
        pltpu.make_async_copy(source, held, load_sems.at[k])
        for k, (source, held) in enumerate(
            ((x_in, x_ref), (wqk_in, wqk), (wv_in, wv), (wout_in, wout), (gain_in, gain_a), (dest_in, dest))
        )
    ]
    for k in (5, 4, 0, 1, 2, 3):
        loads[k].start()
    barrier = pltpu.get_barrier_semaphore()
    pl.semaphore_signal(barrier, inc=1, device_id=lane(FAR_FIRST[0]), device_id_type=MESH)
    for d in CHIPS_FAR_FIRST[:3]:
        pl.semaphore_signal(barrier, inc=1, device_id=chip_at(d), device_id_type=MESH)
    for d in FAR_FIRST[1:]:
        pl.semaphore_signal(barrier, inc=1, device_id=lane(d), device_id_type=MESH)
    for d in CHIPS_FAR_FIRST[3:]:
        pl.semaphore_signal(barrier, inc=1, device_id=chip_at(d), device_id_type=MESH)
    pl.semaphore_signal(barrier, inc=1, device_id=partner, device_id_type=MESH)

    loads[5].wait()
    offsets = [lax.bitwise_and(lax.shift_right_arithmetic(dest[c], 4) - me, LANES - 1) for c in range(CLUSTERS)]
    first, second, active, upto = [], [], [], []
    count = jnp.int32(0)
    for d in range(LANES):
        if d == LANES // 2:
            loads[4].wait()
            loads[0].wait()
        lo, hi = jnp.int32(CLUSTERS), jnp.int32(0)
        for c in range(CLUSTERS):
            hi = jnp.where(offsets[c] == d, c, hi)
            lo = jnp.where(offsets[CLUSTERS - 1 - c] == d, CLUSTERS - 1 - c, lo)
        hit = jnp.where(lo < CLUSTERS, 1, 0)
        count = count + hit
        first.append(jnp.minimum(lo, CLUSTERS - 1))
        second.append(hi)
        active.append(hit)
        upto.append(count)


    for c in range(CLUSTERS):
        normed[c] = norm_rows(x_ref[c * CLUSTER:(c + 1) * CLUSTER, :], gain_a[...])
    for d in range(LANES):
        held = recv if d == 0 else send
        held[2 * d] = normed[first[d]]
        held[2 * d + 1] = normed[second[d]]

    pl.semaphore_wait(barrier, LANES - 1 + CHIPS - 1 + 1)
    for d in FAR_FIRST:
        copy = pltpu.make_async_remote_copy(
            src_ref=send.at[pl.ds(2 * d, 2)], dst_ref=recv.at[pl.ds(2 * d, 2)],
            send_sem=out_sems.at[0], recv_sem=in_sems.at[0], device_id=lane(d), device_id_type=MESH,
        )
        copy.start()

    def head_cols(rows, h):
        start = h % 4 * HEAD
        half = rows[:, h // 4 * 128:(h // 4 + 1) * 128]
        return (pltpu.roll(half, 128 - start, axis=1) if start else half)[:, :HEAD]

    def set_keys(rows):
        for h in range(HEADS):
            keys[h] = head_cols(rows, h)

    def set_values(held, value_t, first_head=0):
        for h in range(value_t.shape[0] // HEAD):
            held[first_head + h, :HEAD, :] = value_t[h * HEAD:(h + 1) * HEAD, :]

    def project(source, query_t):
        states = source[...].reshape(ROWS, C)
        turned = states.T
        query_t[...] = jnp.dot(wqk[:, :C].T, turned, preferred_element_type=F32).astype(BF)
        key_rows = jnp.dot(states, wqk[:, C:], preferred_element_type=F32).astype(BF)
        set_keys(key_rows)
        set_values(vals, jnp.dot(wv[...].T, turned, preferred_element_type=F32).astype(BF))
        return key_rows

    for h in range(HEADS):
        vals[h, HEAD:, :] = jnp.ones((16, ROWS), BF)
        pool_vals[h, HEAD:, :] = jnp.ones((16, ROWS), BF)
    for load in loads[1:3]:
        load.wait()
    key_rows = project(normed, near_q)

    row = lax.broadcasted_iota(jnp.int32, (POOLED, ROWS), 0)
    col = lax.broadcasted_iota(jnp.int32, (POOLED, ROWS), 1)
    pooling = jnp.where(col // POOL == row, 1.0 / math.sqrt(POOL), 0.0).astype(BF)
    pool[:POOLED, :C] = jnp.dot(pooling, key_rows, preferred_element_type=F32).astype(BF)
    value_rows = jnp.dot(normed[...].reshape(ROWS, C), wv[...], preferred_element_type=F32).astype(BF)
    pool[:POOLED, C:] = jnp.dot(pooling, value_rows, preferred_element_type=F32).astype(BF)
    for d in CHIPS_FAR_FIRST:
        copy = pltpu.make_async_remote_copy(
            src_ref=pool.at[pl.ds(0, POOLED)], dst_ref=pool.at[pl.ds(d * POOLED, POOLED)],
            send_sem=pout_sems.at[1], recv_sem=pin_sems.at[1], device_id=chip_at(d), device_id_type=MESH,
        )
        copy.start()

    def attend(query_t, keys, vals, finish, between=None, ready=False, following=None, before_last=None, side=None):
        def spot_of(i):
            return i // QBLOCKS, pl.ds(pl.multiple_of(i % QBLOCKS * QB, QB), QB)

        def head_rows(h):
            return pl.ds(pl.multiple_of(h * HEAD, HEAD), HEAD)

        def scores_of(i, slot, r, top, query_t=query_t, keys=keys):
            h, cols = spot_of(i)
            rows = pl.ds(r * PIECE, PIECE)
            s = jnp.dot(keys[h, rows, :], query_t[head_rows(h), cols], preferred_element_type=F32)
            score[slot, rows, :] = s
            for j in range(PIECE // 8):
                top = jnp.maximum(top, s[j * 8:(j + 1) * 8])
            return top

        def sum_of(h, slot, c, total):
            rows = pl.ds(c * DEPTH, DEPTH)
            return total + jnp.dot(vals[h, :, rows], weight[slot, rows, :], preferred_element_type=F32)

        def top_of(slot):
            return jnp.max(tops[slot], axis=0, keepdims=True)

        low = jnp.full((8, QB), -jnp.inf, F32)
        none = jnp.zeros((48, QB), F32)

        def step(g, even, last=False):
            for b in range(GROUP):
                i = g * GROUP + b
                now = b if even else GROUP + b
                other = GROUP + b if even else b
                old = jnp.maximum(i - GROUP, 0)
                new = jnp.minimum(i + GROUP, BLOCKS - 1)
                old_head, old_cols = spot_of(old)
                head, cols = spot_of(i)
                old_top = top_of(other)
                top = top_of(now)
                new_top, total, last_total = low, none, none
                for r in range(ROWS // PIECE):
                    rows = pl.ds(r * PIECE, PIECE)
                    if not last:
                        new_top = scores_of(new, other, r, new_top)
                    else:
                        if side is not None:
                            side(b * (ROWS // PIECE) + r)
                        if following is not None:
                            new_top = scores_of(b, other, r, new_top, *following)
                    weight[now, rows, :] = jnp.exp2((score[now, rows, :] - top) * SCALE).astype(BF)
                    if (r + 1) * PIECE % DEPTH == 0:
                        part = (r + 1) * PIECE // DEPTH - 1
                        total = sum_of(old_head, other, part, total)
                        if last:
                            last_total = sum_of(head, now, part, last_total)
                finish(old_head, old_cols, old_top, total)
                if last:
                    finish(head, cols, top, last_total)
                if not last or following is not None:
                    tops[other] = new_top

        for b in range(0 if ready else GROUP):
            top = low
            for r in range(ROWS // PIECE):
                top = scores_of(b, b, r, top)
            tops[b] = top

        pairs = BLOCKS // GROUP // 2

        def pair(t, _):
            @pl.when(t < pairs)
            def _():
                step(2 * t, True)

            if between is not None:
                @pl.when(t >= 1)
                def _():
                    between(t - 1)

            @pl.when(t < pairs - 1)
            def _():
                step(2 * t + 1, False)

            if before_last is not None:
                pl.when(t == pairs - 1)(before_last)

            @pl.when(t == pairs - 1)
            def _():
                step(2 * t + 1, False, last=True)

            return 0

        lax.fori_loop(0, pairs, pair, 0)

    def keep(h, cols, top, total):
        near_sum[h, :, cols] = total
        near_max[h, :, cols] = jnp.broadcast_to(top, (8, QB))

    def head_rows(h):
        return pl.ds(pl.multiple_of(h * HEAD, HEAD), HEAD)

    def close(total):
        return (total[:HEAD] / total[HEAD:HEAD + 1]).astype(BF)

    def merge(h, cols, top, total):
        before = near_max[h, :1, cols]
        both = jnp.maximum(before, top)
        whole = near_sum[h, :, cols] * jnp.exp2((before - both) * SCALE) + total * jnp.exp2((top - both) * SCALE)
        near_t[head_rows(h), cols] = close(whole)

    def far_done(h, cols, top, total):
        rows = pl.ds(pl.multiple_of(h % 2 * HEAD, HEAD), HEAD)
        block = close(total)
        for k in range(QB // (2 * CLUSTER)):
            at = h // 2 * (LANES // 2) + cols.start // (2 * CLUSTER) + k
            far_t[at, rows, :] = block[:, k * 2 * CLUSTER:(k + 1) * 2 * CLUSTER]

    attend(near_q, keys, vals, keep)

    pltpu.make_async_remote_copy(
        src_ref=pool.at[pl.ds(POOLED, ROWS // 2 - POOLED)], dst_ref=pool.at[pl.ds(POOLED, ROWS // 2 - POOLED)],
        send_sem=pout_sems.at[1], recv_sem=pin_sems.at[1], device_id=chip_at(1), device_id_type=MESH,
    ).wait()
    across = pltpu.make_async_remote_copy(
        src_ref=pool.at[pl.ds(0, ROWS // 2)], dst_ref=pool.at[pl.ds(ROWS // 2, ROWS // 2)],
        send_sem=pout_sems.at[0], recv_sem=pin_sems.at[0], device_id=partner, device_id_type=MESH,
    )
    across.start()

    picks = []
    for j in range(LANES // 2):
        d = jnp.int32(0)
        for k in range(LANES):
            d = d + jnp.where(upto[k] <= j, 1, 0)
        picks.append(jnp.minimum(d, LANES - 1))

    pltpu.make_async_remote_copy(
        src_ref=send.at[pl.ds(2, 2 * LANES - 2)], dst_ref=recv.at[pl.ds(2, 2 * LANES - 2)],
        send_sem=out_sems.at[0], recv_sem=in_sems.at[0], device_id=lane(1), device_id_type=MESH,
    ).wait()
    for j in range(LANES // 2):
        settled[2 * j] = recv[2 * picks[j]]
        settled[2 * j + 1] = recv[2 * picks[j] + 1]
    project(settled, far_q)
    def back_copy(part, d):
        at = part * LANES + d
        return pltpu.make_async_remote_copy(
            src_ref=back_send.at[at], dst_ref=back_recv.at[at],
            send_sem=bout_sems.at[part], recv_sem=bin_sems.at[part], device_id=lane(-d), device_id_type=MESH,
        )

    def send_back(part):
        for d in range(LANES):
            held = back_recv if d == 0 else back_send
            j = jnp.minimum(upto[d] - active[d], LANES // 2 - 1)
            held[part * LANES + d] = far_t[part * (LANES // 2) + j]
        for d in FAR_FIRST:
            back_copy(part, d).start()

    def pooled_here():
        across.wait()
        pool_keys[0] = head_cols(pool, 0)

    def pooled_layout(k):
        if 1 <= k < HEADS:
            pool_keys[k] = head_cols(pool, k)
        elif k in (HEADS, HEADS + 4):
            first_head = k - HEADS
            set_values(pool_vals, pool[:, C + first_head * HEAD:C + (first_head + 4) * HEAD].T, first_head)

    attend(
        far_q, keys, vals, far_done, send_back,
        following=(near_q, pool_keys), before_last=pooled_here, side=pooled_layout,
    )
    send_back(PARTS - 1)

    def returned():
        for part in range(PARTS):
            rest = pl.ds(part * LANES + 1, LANES - 1)
            pltpu.make_async_remote_copy(
                src_ref=back_send.at[rest], dst_ref=back_recv.at[rest],
                send_sem=bout_sems.at[part], recv_sem=bin_sems.at[part], device_id=lane(1), device_id_type=MESH,
            ).wait()

    def turn_back(k):
        if k < LANES // 2:
            block = jnp.concatenate([back_recv[part * LANES + picks[k]] for part in range(PARTS)], axis=0)
            normed[2 * k:2 * k + 2] = block.T.reshape(2, CLUSTER, C)

    attend(near_q, pool_keys, pool_vals, merge, ready=True, before_last=returned, side=turn_back)
    loads[3].wait()
    for i in range(ROWS // ROW_CHUNK):
        rows = slice(i * ROW_CHUNK, (i + 1) * ROW_CHUNK)
        per_chunk = ROW_CHUNK // CLUSTER
        for c in range(i * per_chunk, (i + 1) * per_chunk):
            at = jnp.int32(0)
            for j in range(LANES // 2 - 1):
                at = at + jnp.where(picks[j] < offsets[c], 2, 0)
            rank = jnp.int32(0)
            for e in range(c):
                rank = rank + jnp.where(offsets[e] == offsets[c], 1, 0)
            settled[c] = normed[at + jnp.minimum(rank, 1)]
        far = settled[i * per_chunk:(i + 1) * per_chunk].reshape(ROW_CHUNK, C)
        out[rows, :] = (
            x_ref[rows, :].astype(F32)
            + jnp.dot(near_t[:, rows].T, wout[...], preferred_element_type=F32)
            + jnp.dot(far, wout[...], preferred_element_type=F32)
        ).astype(BF)


def gelu(x):
    half = 0.5 * x
    inner = x * (GELU_A + GELU_B * (x * x))
    return half + half * jnp.tanh(inner)


def mlp_kernel(after_ref, gain_m, wup, wdown, out):
    after = after_ref[...]
    mlp_in = norm_rows(after, gain_m[...])
    total = after.astype(F32)
    for k in range(MLP_SPLIT):
        cols = pl.ds(k * (HIDDEN // MLP_SPLIT), HIDDEN // MLP_SPLIT)
        hidden = gelu(jnp.dot(mlp_in, wup[:, cols], preferred_element_type=F32)).astype(BF)
        total = total + jnp.dot(hidden, wdown[cols, :], preferred_element_type=F32)
    out[...] = total.astype(BF)


def per_device(points, gain_attn, w_query_key, w_value, w_out, gain_mlp, w_up, w_down, cluster_dest):
    vmem = pl.BlockSpec(memory_space=pltpu.VMEM)
    clusters = pltpu.VMEM((CLUSTERS, CLUSTER, C), BF)
    slots = pltpu.VMEM((2 * LANES, CLUSTER, C), BF)
    turned = pltpu.VMEM((C, ROWS), BF)
    parts = pltpu.VMEM((PARTS * LANES, PART, 2 * CLUSTER), BF)
    anywhere = pl.BlockSpec(memory_space=pltpu.HBM)
    moved = (points.reshape(ROWS, C), w_query_key, w_value, w_out, gain_attn.reshape(1, C), cluster_dest.reshape(CLUSTERS))
    moved = tuple(pltpu.with_memory_space_constraint(a, pltpu.HBM) for a in moved)
    after = pl.pallas_call(
        kernel,
        out_shape=jax.ShapeDtypeStruct((ROWS, C), BF),
        in_specs=[anywhere] * 6,
        out_specs=vmem,
        scratch_shapes=[pltpu.VMEM(a.shape, a.dtype) for a in moved[:-1]]
        + [pltpu.SMEM((CLUSTERS,), jnp.int32)]
        + [
            clusters, clusters,
            turned, turned,
            pltpu.VMEM((HEADS, ROWS, HEAD), BF),
            pltpu.VMEM((HEADS, 48, ROWS), BF),
            pltpu.VMEM((HEADS, ROWS, HEAD), BF),
            pltpu.VMEM((HEADS, 48, ROWS), BF),
            pltpu.VMEM((ROWS, 2 * C), BF),
            pltpu.VMEM((2 * GROUP, ROWS, QB), F32),
            pltpu.VMEM((2 * GROUP, ROWS, QB), BF),
            pltpu.VMEM((2 * GROUP, 8, QB), F32),
            pltpu.VMEM((HEADS, 48, ROWS), F32),
            pltpu.VMEM((HEADS, 8, ROWS), F32),
            turned,
            pltpu.VMEM((PARTS * LANES // 2, PART, 2 * CLUSTER), BF),
            slots, slots, parts, parts,
        ]
        + [pltpu.SemaphoreType.DMA((1,))] * 2
        + [pltpu.SemaphoreType.DMA((PARTS,))] * 2
        + [pltpu.SemaphoreType.DMA((2,))] * 2
        + [pltpu.SemaphoreType.DMA((6,))],
        compiler_params=pltpu.CompilerParams(
            collective_id=0, has_side_effects=True, vmem_limit_bytes=40 * 1024 * 1024
        ),
        name="block",
    )(
        *moved
    )
    rows = pl.BlockSpec((MLP_ROWS, C), lambda i: (i, 0))
    result = pl.pallas_call(
        mlp_kernel,
        grid=(ROWS // MLP_ROWS,),
        out_shape=jax.ShapeDtypeStruct((ROWS, C), BF),
        in_specs=[rows] + [vmem] * 3,
        out_specs=rows,
        compiler_params=pltpu.CompilerParams(vmem_limit_bytes=12 * 1024 * 1024),
        name="mlp",
    )(after, gain_mlp.reshape(1, C), w_up, w_down)
    return result.reshape(points.shape)


def solution(mesh):
    placed = (P("ball", "region", None, None),) + (P(),) * 7 + (P("ball", "region", None),)
    return jax.shard_map(
        per_device, mesh=mesh, in_specs=placed, out_specs=P("ball", "region", None, None), check_vma=False
    )
```
